128 devices in a mesh: tm: 16 (over x, y_hi, core), dom: 8 (over z, y_lo).
Axes of the slice: x: 4, y: 4 (y_hi: 2, y_lo: 2; y = y_hi * 2 + y_lo), z: 4, core: 2. Of those that a mesh axis runs over, the one named last changes fastest.
Arguments:
- state_interior: float32 [16, 16384, 128], P('tm', 'dom'), may hold values from -6 to 6
- state_shared: float32 [16, 2048, 128], P('tm'), may hold values from -6 to 6
- gain_interior: float32 [16, 16384], P('tm', 'dom'), may hold values from 0.2 to 0.95
- gain_shared: float32 [16, 2048], P('tm'), may hold values from 0.2 to 0.95
- jac_blocks: float32 [256, 64, 64], P('dom'), may hold values from -1.5 to 10, as said below
- off_blocks: float32 [256, 64, 64], P('dom'), may hold values from -0.6 to 0.6
- block_link: int32 [256], P('dom'), may hold values from 0 to 31
- mass: float32 [16384], P('dom'), may hold values from 0.5 to 4
- shared_mass: float32 [2048], replicated, may hold values from 0.5 to 2
- shared_diag: float32 [2048], replicated, may hold values from 2.5 to 4
- link_node: int32 [4096], P('dom'), may hold values from 0 to 2047
- link_shared: int32 [4096], P('dom'), may hold values from 0 to 2047
- link_cond: float32 [4096], P('dom'), may hold values from 0.5 to 2
- source_amp: float32 [16384, 128], P('dom'), may hold values from -12 to 12
- phase: float32 [16384], P('dom'), may hold values from -3.140625 to 3.140625
- nonlin: float32 [128], replicated, may hold values from 0.1 to 1
Outputs:
- new_interior: float32 [16, 16384, 128], P('tm', 'dom')
- new_shared: float32 [16, 2048, 128], P('tm')
The draws below stay inside these ranges and needn't reach their ends.
Inputs may be any that keep to these rules, and one draw needn't show every extreme that they name: `jac_blocks`: each block has diagonal entries from 6 to 10 and off-diagonal entries of magnitude at most 1.5.
All inputs are finite; a program needn't handle non-finite values.
Results may differ from the reference program's by a relative error of at most 0.0001.
Values sent between devices are 32-bit elements; how exact they have to be, the bound alone decides.
A program may use at most 128 MiB of HBM per device.

```python
import math
from functools import partial
import jax
import jax.numpy as jnp
from jax import lax

S = 128
BLK = 64
NB_DEV = 32
KI = 512
NS = 2048
FINE = 2
NEWTON = 2
KRYLOV = 2
NODE_DEV = 2048
NODES = 16384
BLOCKS = 256
LINKS = 4096
SLICES = 16


def draw_jac_blocks(key, part):
    first_key, second_key = jax.random.split(jax.random.fold_in(key, 11))
    shape = (BLOCKS, BLK, BLK)
    row_ids = lax.broadcasted_iota(jnp.int32, shape, 1)
    col_ids = lax.broadcasted_iota(jnp.int32, shape, 2)
    offdiag = 0.25 * jnp.clip(jax.random.normal(first_key, shape, jnp.float32), -6.0, 6.0)
    diagonal = jax.random.uniform(second_key, shape, jnp.float32, 6.0, 10.0)
    return jnp.where(row_ids == col_ids, diagonal, offdiag).astype(jnp.float32)


def set_ends(array, own_key, low, largest):
    spot = [jax.random.randint(jax.random.fold_in(own_key, axis), (), 0, length) for axis, length in enumerate(array.shape)]
    widest = array.shape.index(max(array.shape))
    beside = spot[:widest] + [(spot[widest] + 1) % array.shape[widest]] + spot[widest + 1:]
    return array.at[tuple(spot)].set(low).at[tuple(beside)].set(largest)


def block_levels(stream_key, extent, shards, smallest, top_value):
    def one(axis_at, shards_of):
        steps = jax.random.uniform(jax.random.fold_in(jax.random.fold_in(stream_key, 6), axis_at), (shards_of,), jnp.float32, smallest / len(shards), top_value / len(shards))
        return jnp.repeat(jnp.exp(steps), extent[axis_at] // shards_of).reshape((-1,) + (1,) * (len(extent) - axis_at - 1))

    factor_of = one(*shards[0])
    for cut in shards[1:]:
        factor_of = factor_of * one(*cut)
    return factor_of


def scatter_about(key, dims, deviation, reach, pieces=(), kind=jnp.bfloat16):
    result = jax.random.normal(key, dims, jnp.float32) * deviation
    if len(pieces) > 0:
        result = block_levels(key, dims, pieces, -0.22, 0.18) * result
    return jnp.clip(result, min=-reach, max=reach).astype(kind)


def setup_inputs(seed: int = 0) -> dict:
    seeds = jax.random.split(jax.random.key(seed), 17)
    return {
        "state_interior": scatter_about(seeds[0], (SLICES, NODES, S), 1.0, 6.0, ((0, 16), (1, 8)), jnp.float32),
        "state_shared": scatter_about(seeds[1], (SLICES, NS, S), 1.0, 6.0, ((0, 16),), jnp.float32),
        "gain_interior": jnp.clip(0.2 + 0.75 * jax.random.uniform(seeds[2], (SLICES, NODES), jnp.float32) ** block_levels(seeds[2], (SLICES, NODES), ((0, 16), (1, 8)), -0.2, 0.2), 0.2, 0.95),
        "gain_shared": jnp.clip(0.2 + 0.75 * jax.random.uniform(seeds[3], (SLICES, NS), jnp.float32) ** block_levels(seeds[3], (SLICES, NS), ((0, 16),), -0.2, 0.2), 0.2, 0.95),
        "jac_blocks": draw_jac_blocks(jax.random.fold_in(seeds[16], 71), 0),
        "off_blocks": scatter_about(seeds[5], (BLOCKS, BLK, BLK), 0.1, 0.6, ((0, 8),), jnp.float32),
        "block_link": set_ends(jax.random.randint(seeds[6], (BLOCKS,), 0, NB_DEV), jax.random.fold_in(seeds[6], 1), 0, NB_DEV - 1).astype(jnp.int32),
        "mass": jnp.clip(jnp.exp(math.log(4.0) - 2.0794415 * jax.random.uniform(seeds[7], (NODES,), jnp.float32) ** block_levels(seeds[7], (NODES,), ((0, 8),), -0.2, 0.2)), 0.5, 4.0),
        "shared_mass": jnp.clip(jnp.exp(jax.random.uniform(seeds[8], (NS,), jnp.float32, math.log(0.5), math.log(2.0))), 0.5, 2.0),
        "shared_diag": jnp.clip(jax.random.uniform(seeds[9], (NS,), jnp.float32, 2.5, 4.0), 2.5, 4.0),
        "link_node": set_ends(jax.random.randint(seeds[10], (LINKS,), 0, NODE_DEV), jax.random.fold_in(seeds[10], 1), 0, NODE_DEV - 1).astype(jnp.int32),
        "link_shared": set_ends(jax.random.randint(seeds[11], (LINKS,), 0, NS), jax.random.fold_in(seeds[11], 1), 0, NS - 1).astype(jnp.int32),
        "link_cond": jnp.clip(jnp.exp(math.log(2.0) - 1.3862944 * jax.random.uniform(seeds[12], (LINKS,), jnp.float32) ** block_levels(seeds[12], (LINKS,), ((0, 8),), -0.2, 0.2)), 0.5, 2.0),
        "source_amp": scatter_about(seeds[13], (NODES, S), 2.0, 12.0, ((0, 8),), jnp.float32),
        "phase": jnp.clip(jax.random.uniform(seeds[14], (NODES,), jnp.float32, -3.140625, 3.140625), -3.140625, 3.140625),
        "nonlin": jnp.clip(jnp.exp(jax.random.uniform(seeds[15], (S,), jnp.float32, math.log(0.1), math.log(1.0))), 0.1, 1.0),
    }


def rotate_solve(columns, start_norm, krylov):
    cosines = []
    sine_parts = []
    rhs_vals = [start_norm] + [jnp.zeros_like(start_norm) for j in range(krylov)]
    triangle = []
    for j in range(krylov):
        column = list(columns[j])
        for i in range(j):
            upper_entry = cosines[i] * column[i] + sine_parts[i] * column[i + 1]
            lower_entry = -sine_parts[i] * column[i] + cosines[i] * column[i + 1]
            column[i] = upper_entry
            column[i + 1] = lower_entry
        radius = jnp.sqrt(column[j] * column[j] + column[j + 1] * column[j + 1])
        cosine = column[j] / radius
        sine_part = column[j + 1] / radius
        column[j] = radius
        cosines.append(cosine)
        sine_parts.append(sine_part)
        rhs_vals[j + 1] = -sine_part * rhs_vals[j]
        rhs_vals[j] = cosine * rhs_vals[j]
        triangle.append(column[:j + 1])
    coeffs = [None] * krylov
    for j in reversed(range(krylov)):
        partial_rhs = rhs_vals[j]
        for k in range(j + 1, krylov):
            partial_rhs = partial_rhs - triangle[k][j] * coeffs[k]
        coeffs[j] = partial_rhs / triangle[j][j]
    return coeffs

def project_plain(inner_sums, basis_in, basis_sh, image_in, image_sh):
    heights = inner_sums(basis_in, basis_sh, image_in, image_sh)
    for i in range(len(basis_in)):
        image_in = image_in - heights[i] * basis_in[i]
        image_sh = image_sh - heights[i] * basis_sh[i]
    length = jnp.sqrt(inner_sums([image_in], [image_sh], image_in, image_sh)[0])
    return (heights, image_in, image_sh, length)

def krylov_solve(operate_on, inner_sums, project, rhs_in, rhs_sh):
    start_norm = jnp.sqrt(inner_sums([rhs_in], [rhs_sh], rhs_in, rhs_sh)[0] + 1e-30)
    basis_in = [rhs_in / start_norm]
    basis_sh = [rhs_sh / start_norm]
    columns = []
    for j in range(KRYLOV):
        image_in, image_sh = operate_on(basis_in[j], basis_sh[j])
        heights, image_in, image_sh, length = project(basis_in, basis_sh, image_in, image_sh)
        columns.append([heights[i] for i in range(j + 1)] + [length])
        if j + 1 < KRYLOV:
            basis_in.append(image_in / length)
            basis_sh.append(image_sh / length)
    coeffs = rotate_solve(columns, start_norm, KRYLOV)
    step_in = coeffs[0] * basis_in[0]
    step_sh = coeffs[0] * basis_sh[0]
    for j in range(1, KRYLOV):
        step_in = step_in + coeffs[j] * basis_in[j]
        step_sh = step_sh + coeffs[j] * basis_sh[j]
    return (step_in, step_sh)

def propagate(start_in, start_sh, slice_f, slices, operate_on, inner_sums, project, mass, shared_mass, source_amp, phase, nonlin):
    old_in, old_sh = (start_in, start_sh)
    for k in range(FINE):
        angle = (slice_f * FINE + (k + 1.0)) * (2.0 * math.pi / (slices * FINE))
        drive = source_amp * jnp.sin(angle + phase)[:, None]
        fixed_in = mass[:, None] * old_in + drive
        fixed_sh = shared_mass[:, None] * old_sh
        guess_in, guess_sh = (old_in, old_sh)
        for m in range(NEWTON):
            lin_in, lin_sh = operate_on(guess_in, guess_sh)
            resid_in = lin_in + nonlin[None, :] * jnp.tanh(guess_in) - fixed_in
            resid_sh = lin_sh - fixed_sh
            step_in, step_sh = krylov_solve(operate_on, inner_sums, project, -resid_in, -resid_sh)
            guess_in = guess_in + step_in
            guess_sh = guess_sh + step_sh
        old_in, old_sh = (guess_in, guess_sh)
    return (old_in, old_sh)

def compose_maps(earlier, later):
    return (later[0] * earlier[0], later[1] * earlier[1], later[0][:, None] * earlier[2] + later[2], later[1][:, None] * earlier[3] + later[3])

def reference(state_interior, state_shared, gain_interior, gain_shared, jac_blocks, off_blocks, block_link, mass, shared_mass, shared_diag, link_node, link_shared, link_cond, source_amp, phase, nonlin):
    highest = lax.Precision.HIGHEST
    global_link = block_link + jnp.arange(BLOCKS, dtype=jnp.int32) // NB_DEV * NB_DEV
    global_node = link_node + jnp.arange(LINKS, dtype=jnp.int32) // KI * NODE_DEV

    def operate_on(vec_in, vec_sh):
        blocked = vec_in.reshape(BLOCKS, BLK, S)
        block_out = jnp.einsum('bij,bjs->bis', jac_blocks, blocked, precision=highest)
        block_out = block_out + jnp.einsum('bij,bjs->bis', off_blocks, blocked[global_link], precision=highest)
        out_in = block_out.reshape(NODES, S)
        link_flow = link_cond[:, None] * (vec_in[global_node] - vec_sh[link_shared])
        out_in = out_in.at[global_node].add(link_flow)
        out_sh = shared_diag[:, None] * vec_sh - jax.ops.segment_sum(link_flow, link_shared, num_segments=NS)
        return (out_in, out_sh)

    def inner_sums(vecs_in, vecs_sh, other_in, other_sh):
        part_in = jnp.stack([lax.optimization_barrier(jnp.sum(v * other_in, axis=0)) for v in vecs_in])
        part_sh = jnp.stack([lax.optimization_barrier(jnp.sum(v * other_sh, axis=0)) for v in vecs_sh])
        return part_in + part_sh
    project = partial(project_plain, inner_sums)

    def one_slice(packed):
        start_in, start_sh, index = packed
        return propagate(start_in, start_sh, index.astype(jnp.float32), SLICES, operate_on, inner_sums, project, mass, shared_mass, source_amp, phase, nonlin)
    fine_in, fine_sh = lax.map(one_slice, (state_interior, state_shared, jnp.arange(SLICES, dtype=jnp.int32)))
    jump_in = fine_in - gain_interior[:, :, None] * state_interior
    jump_sh = fine_sh - gain_shared[:, :, None] * state_shared
    maps = (gain_interior, gain_shared, jump_in, jump_sh)
    init = (jnp.ones((NODES,), jnp.float32), jnp.ones((NS,), jnp.float32), jnp.zeros((NODES, S), jnp.float32), jnp.zeros((NS, S), jnp.float32))
    totals, unused = lax.scan(lambda carry, item: (compose_maps(carry, item), None), init, maps)
    first_in = totals[2] / (1.0 - totals[0])[:, None]
    first_sh = totals[3] / (1.0 - totals[1])[:, None]

    def advance(carry, item):
        value_in, value_sh = carry
        nxt = (item[0][:, None] * value_in + item[2], item[1][:, None] * value_sh + item[3])
        return (nxt, carry)
    unused_last, values = lax.scan(advance, (first_in, first_sh), maps)
    return (values[0], values[1])
```

```python
import functools
import math

import jax
import jax.numpy as jnp
from jax import lax
from jax.experimental import pallas as pl
from jax.experimental.pallas import tpu as pltpu
from jax.sharding import PartitionSpec as P

FINE = 2
NEWTON = 2
SHIFT = 8.0
LANES = 128
MESH = pl.DeviceIdType.MESH
F32 = jnp.float32
BF16 = jnp.bfloat16

COL_MASS, COL_SIN, COL_GAIN, COL_SHARED, COL_NODE, COL_LINK, COL_COND = 0, 16, 48, 64, 72, 80, 88
FLOW_G, FLOW_P, BACK_P, BACK_Q, SETUP, GRAM, LAST = range(7)


def halves(acc):
    return acc[:, :LANES] + acc[:, LANES:]


def split(value):
    high = value.astype(BF16)
    low = (value - high.astype(F32)).astype(BF16)
    return jnp.concatenate([high, low], axis=1)


def dot(a, b):
    return jnp.dot(a, b, preferred_element_type=F32)


def ones_where(mask):
    return jnp.where(mask, 1.0, 0.0).astype(BF16)


def kernel(
    cap,
    width,
    n_tm,
    n_dom,
    x0_ref,
    w0_ref,
    gain_in_ref,
    gain_sh_ref,
    jac_ref,
    off_ref,
    block_link_ref,
    mass_ref,
    shared_mass_ref,
    shared_diag_ref,
    node_ref,
    link_ref,
    link_smem,
    cond_ref,
    amp_ref,
    phase_ref,
    nonlin_ref,
    out_in_ref,
    out_sh_ref,
    flag_ref,
    x,
    jx,
    g,
    p,
    q,
    fixed,
    flow,
    g_parts,
    p_parts,
    flow_parts,
    slot_parts,
    blocks,
    node_rows,
    node_cols,
    pack,
    unpack,
    own,
    own_t,
    table,
    table_t,
    table2_t,
    link_mass,
    link_cond,
    diag_sh,
    stage,
    recv,
    set_send,
    set_recv,
    gain_send,
    gain_recv,
    gram_send,
    gram_recv,
    jump_send,
    jump_recv,
    value_send,
    value_sh,
    send_sem,
    recv_sem,
    tm_send,
    tm_recv,
):
    me_t, me_d = lax.axis_index("tm"), lax.axis_index("dom")
    nodes = x0_ref.shape[0]
    shard = w0_ref.shape[0] // n_dom
    links = flow.shape[0]
    chunks, shard_chunks, link_chunks = nodes // LANES, shard // LANES, links // LANES
    at_sh, at_link = nodes, nodes + shard
    per_owner = width // LANES
    nblocks, bsize = jac_ref.shape[0], jac_ref.shape[1]
    iota0 = lax.broadcasted_iota(jnp.int32, (LANES, LANES), 0)
    iota1 = lax.broadcasted_iota(jnp.int32, (LANES, LANES), 1)

    def rows(start, size):
        return pl.ds(pl.multiple_of(start, size), size)

    def dom_peer(step):
        return lax.rem(me_d + step, n_dom)

    def dom_source(step):
        return lax.rem(me_d + n_dom - step, n_dom)

    def tm_peer(step):
        return lax.rem(me_t + step, n_tm)

    def tm_source(step):
        return lax.rem(me_t + n_tm - step, n_tm)

    def dom_copy(kind, step, source, target):
        return pltpu.make_async_remote_copy(
            src_ref=source,
            dst_ref=target,
            send_sem=send_sem.at[kind, step],
            recv_sem=recv_sem.at[kind, step],
            device_id={"dom": dom_peer(step)},
            device_id_type=MESH,
        )

    def tm_copy(kind, step, source, target):
        return pltpu.make_async_remote_copy(
            src_ref=source,
            dst_ref=target,
            send_sem=tm_send.at[kind, step],
            recv_sem=tm_recv.at[kind, step],
            device_id={"tm": tm_peer(step)},
            device_id_type=MESH,
        )

    if cap < width:
        for kind in range(4):
            for o in range(n_dom):
                recv[kind, o, cap:, :] = jnp.zeros((width - cap, LANES), F32)
    barrier = pltpu.get_barrier_semaphore()
    for step in range(1, n_dom):
        pl.semaphore_signal(barrier, inc=1, device_id={"dom": dom_peer(step)}, device_id_type=MESH)
    for step in range(1, n_tm):
        pl.semaphore_signal(barrier, inc=1, device_id={"tm": tm_peer(step)}, device_id_type=MESH)

    slice_f = me_t.astype(F32)
    table[...] = jnp.zeros((LANES, LANES), F32)
    table[COL_MASS : COL_MASS + chunks, :] = mass_ref[...]
    for k in range(FINE):
        angle = (slice_f * FINE + (k + 1.0)) * (2.0 * math.pi / (n_tm * FINE))
        at = COL_SIN + chunks * k
        table[at : at + chunks, :] = jnp.sin(angle + phase_ref[...])
    table[COL_GAIN : COL_GAIN + chunks, :] = gain_in_ref[...]
    for a in range(shard_chunks):
        row = shard_chunks * me_d + a
        table[COL_SHARED + a : COL_SHARED + a + 1, :] = shared_mass_ref[pl.ds(row, 1), :]
        table[COL_SHARED + 2 + a : COL_SHARED + 3 + a, :] = shared_diag_ref[pl.ds(row, 1), :]
        table[COL_SHARED + 4 + a : COL_SHARED + 5 + a, :] = gain_sh_ref[pl.ds(row, 1), :]
    table[COL_NODE : COL_NODE + link_chunks, :] = node_ref[...].astype(F32)
    table[COL_LINK : COL_LINK + link_chunks, :] = link_ref[...].astype(F32)
    table[COL_COND : COL_COND + link_chunks, :] = cond_ref[...]
    table_t[...] = table[...].T

    def column(at):
        return table_t[:, at : at + 1]

    link_col = [column(COL_LINK + j).astype(jnp.int32) for j in range(link_chunks)]
    link_row = [link_ref[j : j + 1, :] for j in range(link_chunks)]
    if cap == width:
        slot_col, slot_row = link_col, link_row
        crowd = jnp.zeros((1, LANES), F32)
    else:
        owner_col = [v // shard for v in link_col]
        owner_row = [v // shard for v in link_row]
        slot_col, slot_row = [], []
        crowd = jnp.zeros((1, LANES), F32)
        for j in range(link_chunks):
            rank_row = jnp.zeros((1, LANES), F32)
            rank_col = jnp.zeros((LANES, 1), F32)
            for i in range(j + 1):
                same_row = owner_col[i] == owner_row[j]
                same_col = owner_col[j] == owner_row[i]
                if i == j:
                    same_row = same_row & (iota0 < iota1)
                    same_col = same_col & (iota1 < iota0)
                rank_row += jnp.sum(jnp.where(same_row, 1.0, 0.0), axis=0, keepdims=True)
                rank_col += jnp.sum(jnp.where(same_col, 1.0, 0.0), axis=1, keepdims=True)
            crowd = jnp.maximum(crowd, rank_row)
            slot_row.append(owner_row[j] * width + rank_row.astype(jnp.int32))
            slot_col.append(owner_col[j] * width + rank_col.astype(jnp.int32))
    set_send[...] = jnp.zeros(set_send.shape, F32)
    for i in range(n_dom * per_owner):
        held = jnp.full((1, LANES), -1.0, F32)
        total = jnp.zeros((1, LANES), F32)
        for j in range(link_chunks):
            here = (iota1 + LANES * i) == slot_col[j]
            local = (link_col[j] % shard).astype(F32)
            held = jnp.maximum(held, jnp.max(jnp.where(here, local, -1.0), axis=0, keepdims=True))
            total += jnp.sum(jnp.where(here, column(COL_COND + j), 0.0), axis=0, keepdims=True)
            unpack[LANES * j : LANES * (j + 1), LANES * i : LANES * (i + 1)] = ones_where(here)
            pack[LANES * i : LANES * (i + 1), LANES * j : LANES * (j + 1)] = ones_where(
                (iota0 + LANES * i) == slot_row[j]
            )
        o, h = i // per_owner, i % per_owner
        set_send[o, h : h + 1, :] = held
        set_send[o, 2 + h : 3 + h, :] = total
    for o in range(n_dom):
        set_send[o, 4:5, :] = crowd
    gain_send[...] = jnp.zeros(gain_send.shape, F32)
    for m in range(n_tm):
        gain_send[m, 0:1, :] = gain_in_ref[m : m + 1, :]
        row = shard_chunks * me_d + m * shard_chunks // n_tm
        gain_send[m, 1:2, :] = gain_sh_ref[pl.ds(row, 1), :]

    pl.semaphore_wait(barrier, n_dom - 1 + n_tm - 1)
    for step in range(1, n_dom):
        dom_copy(SETUP, step, set_send.at[dom_peer(step)], set_recv.at[me_d]).start()
    for step in range(1, n_tm):
        tm_copy(0, step, gain_send.at[tm_peer(step)], gain_recv.at[me_t]).start()
    set_recv[me_d] = set_send[me_d]
    gain_recv[me_t] = gain_send[me_t]

    for j in range(link_chunks):
        node_row = node_ref[j : j + 1, :]
        node_col = column(COL_NODE + j).astype(jnp.int32)
        link_cond[LANES * j : LANES * (j + 1), :] = jnp.broadcast_to(column(COL_COND + j), (LANES, LANES))
        across = slice(LANES * j, LANES * (j + 1))

        def select(i, carry):
            base = pl.multiple_of(i * LANES, LANES)
            node_rows[pl.ds(base, LANES), across] = ones_where(iota0 + base == node_row)
            node_cols[across, pl.ds(base, LANES)] = ones_where(iota1 + base == node_col)
            return carry

        lax.fori_loop(0, chunks, select, 0, unroll=2)
        mass_sum = jnp.zeros((LANES, LANES), F32)
        for i in range(w0_ref.shape[0] // LANES):
            mass_sum += jnp.where(iota1 + LANES * i == link_col[j], shared_mass_ref[i : i + 1, :], 0.0)
        link_mass[across, :] = jnp.broadcast_to(jnp.sum(mass_sum, axis=1, keepdims=True), (LANES, LANES))

    def cut(b, carry):
        blocks[b] = split(jnp.concatenate([jac_ref[b], off_ref[b]], axis=1))
        return carry

    lax.fori_loop(0, nblocks, cut, 0, unroll=2)

    each = LANES // bsize

    def begin(i, carry):
        at = rows(i * LANES, LANES)
        value = x0_ref[at, :]
        x[at, :] = value
        g_parts[pl.ds(i * each, each)] = split(value).reshape(each, bsize, 2 * LANES)
        return carry

    lax.fori_loop(0, chunks, begin, 0)
    x[at_sh : at_sh + shard, :] = w0_ref[rows(me_d * shard, shard), :]

    def fetch(l, carry):
        x[pl.ds(at_link + l, 1), :] = w0_ref[pl.ds(link_smem[l // LANES, lax.rem(l, LANES)], 1), :]
        return carry

    lax.fori_loop(0, links, fetch, 0, unroll=8)

    for step in range(1, n_dom):
        dom_copy(SETUP, step, set_send.at[dom_peer(step)], set_recv.at[dom_source(step)]).wait_recv()
    for o in range(n_dom):
        for h in range(per_owner):
            at = o * per_owner + h
            table[at : at + 1, :] = set_recv[o, h : h + 1, :]
    table2_t[...] = table[...].T
    sums = [jnp.zeros((LANES, LANES), F32) for a in range(shard_chunks)]
    crowd = jnp.zeros((1, LANES), F32)
    for o in range(n_dom):
        crowd = jnp.maximum(crowd, set_recv[o, 4:5, :])
        for h in range(per_owner):
            i = o * per_owner + h
            held_row = set_recv[o, h : h + 1, :].astype(jnp.int32)
            held_col = table2_t[:, i : i + 1].astype(jnp.int32)
            for a in range(shard_chunks):
                here = (iota0 + LANES * a) == held_row
                sums[a] += jnp.where(here, set_recv[o, 2 + h : 3 + h, :], 0.0)
                own[LANES * a : LANES * (a + 1), LANES * i : LANES * (i + 1)] = ones_where(here)
                own_t[LANES * i : LANES * (i + 1), LANES * a : LANES * (a + 1)] = ones_where(
                    (iota1 + LANES * a) == held_col
                )
    for a in range(shard_chunks):
        total = column(COL_SHARED + 2 + a) + jnp.sum(sums[a], axis=1, keepdims=True)
        diag_sh[LANES * a : LANES * (a + 1), :] = jnp.broadcast_to(total, (LANES, LANES))
    flag_ref[...] = jnp.broadcast_to(crowd, flag_ref.shape)

    def apply_blocks(parts, out):
        def one(b, carry):
            other = block_link_ref[b]
            mine, theirs = parts[b], parts[other]
            acc = dot(blocks[b], jnp.concatenate([mine, theirs, mine, theirs], axis=0))
            out[rows(b * bsize, bsize), :] = halves(acc)
            return carry

        lax.fori_loop(0, nblocks, one, 0, unroll=4)

    def gather_flow(parts):
        flow[...] = halves(dot(node_cols[...], parts[...].reshape(nodes, 2 * LANES))) * link_cond[...]

    def add_flow(vec, out, shift_by=None, parts=None):
        flow_parts[...] = split(flow[...] - link_cond[...] * vec[at_link : at_link + links, :])
        size = 2 * LANES

        def one(i, carry):
            at = rows(i * size, size)
            value = out[at, :] + halves(dot(node_rows[at, :], flow_parts[...]))
            if shift_by is not None:
                value = value - SHIFT * shift_by[at, :]
            out[at, :] = value
            if parts is not None:
                parts[pl.ds(i * 2 * each, 2 * each)] = split(value).reshape(2 * each, bsize, 2 * LANES)
            return carry

        lax.fori_loop(0, nodes // size, one, 0)

    def start_exchange(kind):
        for step in range(1, n_dom):
            dom_copy(
                kind,
                step,
                stage.at[kind, dom_peer(step), pl.ds(0, cap)],
                recv.at[kind, me_d, pl.ds(0, cap)],
            ).start()
        recv[kind, me_d] = stage[kind, me_d]

    def wait_exchange(kind, receive):
        for step in range(1, n_dom):
            copy = dom_copy(
                kind,
                step,
                stage.at[kind, dom_peer(step), pl.ds(0, cap)],
                recv.at[kind, dom_source(step), pl.ds(0, cap)],
            )
            if receive:
                copy.wait_recv()
            else:
                copy.wait_send()

    def send_flow(kind):
        flow_parts[...] = split(flow[...])

        def one(o, carry):
            stage[kind, o] = halves(dot(pack[rows(o * width, width), :], flow_parts[...]))
            return carry

        lax.fori_loop(0, n_dom, one, 0)
        start_exchange(kind)

    def load_slots(kind):
        for o in range(n_dom):
            slot_parts[o * width : (o + 1) * width, :] = split(recv[kind, o])

    def collect_flow(kind):
        wait_exchange(kind, True)
        load_slots(kind)
        return halves(dot(own[...], slot_parts[...]))

    def send_back(kind, value):
        value_parts = split(value)

        def one(o, carry):
            stage[kind, o] = halves(dot(own_t[rows(o * width, width), :], value_parts))
            return carry

        lax.fori_loop(0, n_dom, one, 0)
        start_exchange(kind)

    def take_back(kind, out):
        wait_exchange(kind, True)
        load_slots(kind)
        out[at_link : at_link + links, :] = halves(dot(unpack[...], slot_parts[...]))

    def set_fixed(k):
        for i in range(chunks):
            at = slice(LANES * i, LANES * (i + 1))
            drive = amp_ref[at, :] * column(COL_SIN + chunks * k + i)
            fixed[at, :] = column(COL_MASS + i) * x[at, :] + drive
        for a in range(shard_chunks):
            at = slice(at_sh + LANES * a, at_sh + LANES * (a + 1))
            fixed[at, :] = column(COL_SHARED + a) * x[at, :]
        fixed[at_link:, :] = link_mass[...] * x[at_link:, :]

    def new_residual():
        def one(i, carry):
            at = rows(i * LANES, LANES)
            value = fixed[at, :] - jx[at, :] - nonlin_ref[...] * jnp.tanh(x[at, :])
            g[at, :] = value
            g_parts[pl.ds(i * each, each)] = split(value).reshape(each, bsize, 2 * LANES)
            return carry

        lax.fori_loop(0, chunks, one, 0)
        g[nodes:, :] = fixed[nodes:, :] - jx[nodes:, :]

    gather_flow(g_parts)
    send_flow(FLOW_G)
    apply_blocks(g_parts, jx)
    add_flow(x, jx)
    set_fixed(0)
    at = slice(at_sh, at_sh + shard)
    wait_exchange(FLOW_G, False)
    jx[at, :] = diag_sh[...] * x[at, :] - collect_flow(FLOW_G)
    send_back(BACK_P, jx[at, :])
    take_back(BACK_P, jx)
    wait_exchange(BACK_P, False)
    new_residual()

    def gram_row(index, total):
        return total[index : index + 1, :]

    def newton(turn, carry):
        gather_flow(g_parts)
        send_flow(FLOW_G)
        apply_blocks(g_parts, p)
        add_flow(g, p, g, p_parts)
        gather_flow(p_parts)
        send_flow(FLOW_P)
        apply_blocks(p_parts, q)
        p[at, :] = (diag_sh[...] - SHIFT) * g[at, :] - collect_flow(FLOW_G)
        send_back(BACK_P, p[at, :])
        q[at, :] = diag_sh[...] * p[at, :] - collect_flow(FLOW_P)
        send_back(BACK_Q, q[at, :])
        take_back(BACK_P, p)
        add_flow(p, q)

        def gram(i, sums):
            here = rows(i * LANES, LANES)
            vg, vp, vq = g[here, :], p[here, :], q[here, :]
            pairs = ((vg, vg), (vg, vp), (vp, vp), (vg, vq), (vp, vq), (vq, vq))
            return tuple(
                s + jnp.sum((a * b).reshape(LANES // 8, 8, LANES), axis=0)
                for s, (a, b) in zip(sums, pairs)
            )

        zero = jnp.zeros((8, LANES), F32)
        sums = lax.fori_loop(0, chunks + shard_chunks, gram, (zero,) * 6)
        for i, s in enumerate(sums):
            gram_send[i : i + 1, :] = jnp.sum(s, axis=0, keepdims=True)
        gram_send[6:8, :] = jnp.zeros((2, LANES), F32)
        for step in range(1, n_dom):
            dom_copy(GRAM, step, gram_send, gram_recv.at[me_d]).start()
        gram_recv[me_d] = gram_send[...]
        for kind in (FLOW_G, FLOW_P, BACK_P, BACK_Q):
            wait_exchange(kind, False)
        for step in range(1, n_dom):
            copy = dom_copy(GRAM, step, gram_send, gram_recv.at[dom_source(step)])
            copy.wait_send()
            copy.wait_recv()
        total = gram_recv[0]
        for o in range(1, n_dom):
            total = total + gram_recv[o]
        gg, gp, pp, gq, pq, qq = [total[i : i + 1, :] for i in range(6)]
        norm2 = gg + 1e-30
        inv2 = 1.0 / norm2
        h00 = (gp + SHIFT * gg) * inv2
        turnover = h00 - SHIFT
        tail2 = pp - 2.0 * turnover * gp + turnover * turnover * gg
        inv_both = 1.0 / (jnp.sqrt(norm2) * jnp.sqrt(tail2))
        inv_tail2 = 1.0 / tail2
        push = turnover * SHIFT
        g_s = gq - turnover * gp - push * gg
        p_s = pq - turnover * pp - push * gp
        q_s = qq - turnover * pq - push * gq
        t_s = p_s - turnover * g_s
        s_s = q_s - turnover * p_s - push * g_s
        g_t = gp - turnover * gg
        h10 = tail2 * inv_both
        h01 = g_s * inv_both
        h11 = t_s * inv_tail2
        h21_2 = (
            s_s * inv_tail2
            - h01 * h01 * (2.0 - gg * inv2)
            - h11 * h11
            + 2.0 * h01 * h11 * g_t * inv_both
        )
        n11 = h00 * h00 + h10 * h10
        n12 = h00 * h01 + h10 * h11
        n22 = h01 * h01 + h11 * h11 + h21_2
        inv_det = 1.0 / (n11 * n22 - n12 * n12)
        c_p = norm2 * inv_both * (h01 * n11 - h00 * n12) * inv_det
        c_g = (h00 * n22 - h01 * n12) * inv_det - turnover * c_p

        def advance(here):
            vg, vp = g[here, :], p[here, :]
            x[here, :] = x[here, :] + c_g * vg + c_p * vp
            jx[here, :] = jx[here, :] + c_g * (vp + SHIFT * vg) + c_p * q[here, :]

        def one(i, carry):
            advance(rows(i * LANES, LANES))
            return carry

        lax.fori_loop(0, chunks + shard_chunks, one, 0)
        take_back(BACK_Q, q)
        advance(slice(at_link, at_link + links))

        @pl.when(turn == NEWTON - 1)
        def _():
            set_fixed(1)

        @pl.when(turn < FINE * NEWTON - 1)
        def _():
            new_residual()

        return carry

    lax.fori_loop(0, FINE * NEWTON, newton, 0)

    per_rows, per_shared = nodes // n_tm, shard // n_tm
    for i in range(chunks):
        here = slice(LANES * i, LANES * (i + 1))
        jump_send[i, :per_rows, :] = x[here, :] - column(COL_GAIN + i) * x0_ref[here, :]
    for a in range(shard_chunks):
        here = slice(at_sh + LANES * a, at_sh + LANES * (a + 1))
        start = w0_ref[rows(me_d * shard + LANES * a, LANES), :]
        jump = x[here, :] - column(COL_SHARED + 4 + a) * start
        pieces = LANES // per_shared
        for m in range(pieces):
            jump_send[a * pieces + m, per_rows:, :] = jump[per_shared * m : per_shared * (m + 1), :]
    for step in range(1, n_tm):
        tm_copy(1, step, jump_send.at[tm_peer(step)], jump_recv.at[me_t]).start()
    jump_recv[me_t] = jump_send[me_t]
    for step in range(1, n_tm):
        tm_copy(0, step, gain_send.at[tm_peer(step)], gain_recv.at[tm_source(step)]).wait_recv()
    for m in range(n_tm):
        table[m : m + 1, :] = gain_recv[m, 0:1, :]
        table[n_tm + m : n_tm + m + 1, :] = gain_recv[m, 1:2, :]
    table2_t[...] = table[...].T
    my_shared = rows(lax.rem(me_t, LANES // per_shared) * per_shared, per_shared)
    for step in range(1, n_tm):
        tm_copy(1, step, jump_send.at[tm_peer(step)], jump_recv.at[tm_source(step)]).wait_recv()
    for part, gains in (
        (slice(0, per_rows), [table2_t[:, m : m + 1] for m in range(n_tm)]),
        (
            slice(per_rows, per_rows + per_shared),
            [table2_t[my_shared, n_tm + m : n_tm + m + 1] for m in range(n_tm)],
        ),
    ):
        whole, total = gains[0], jump_recv[0, part, :]
        for m in range(1, n_tm):
            whole = whole * gains[m]
            total = gains[m] * total + jump_recv[m, part, :]
        value = total / (1.0 - whole)
        for m in range(n_tm):
            value_send[m, part, :] = value
            if m + 1 < n_tm:
                value = gains[m] * value + jump_recv[m, part, :]

    def value_copy(step, holder):
        source = value_send.at[tm_peer(step), pl.ds(0, per_rows)]
        return tm_copy(2, step, source, out_in_ref.at[rows(holder * per_rows, per_rows)])

    def shared_copy(step, holder):
        source = value_send.at[tm_peer(step), pl.ds(per_rows, per_shared)]
        return tm_copy(3, step, source, value_sh.at[rows(holder * per_shared, per_shared)])

    for step in range(1, n_tm):
        shared_copy(step, me_t).start()
        value_copy(step, me_t).start()
    out_in_ref[rows(me_t * per_rows, per_rows), :] = value_send[me_t, :per_rows, :]
    value_sh[rows(me_t * per_shared, per_shared), :] = value_send[me_t, per_rows:, :]
    for step in range(1, n_tm):
        shared_copy(step, tm_source(step)).wait_recv()
    for step in range(1, n_dom):
        dom_copy(LAST, step, value_sh, out_sh_ref.at[rows(me_d * shard, shard)]).start()
    out_sh_ref[rows(me_d * shard, shard), :] = value_sh[...]
    for step in range(1, n_tm):
        value_copy(step, tm_source(step)).wait_recv()
    for step in range(1, n_dom):
        copy = dom_copy(LAST, step, value_sh, out_sh_ref.at[rows(dom_source(step) * shard, shard)])
        copy.wait_recv()
        copy.wait_send()
        dom_copy(SETUP, step, set_send.at[dom_peer(step)], set_recv.at[me_d]).wait_send()
    for step in range(1, n_tm):
        tm_copy(0, step, gain_send.at[tm_peer(step)], gain_recv.at[me_t]).wait_send()
        tm_copy(1, step, jump_send.at[tm_peer(step)], jump_recv.at[me_t]).wait_send()
        shared_copy(step, me_t).wait_send()
        value_copy(step, me_t).wait_send()


def run(cap, width, collective_id, n_tm, n_dom, operands):
    nodes, samples = operands[0].shape
    shared = operands[1].shape[0]
    shard = shared // n_dom
    links = operands[10].shape[0] * operands[10].shape[1]
    nblocks, bsize = operands[4].shape[0], operands[4].shape[1]
    total = nodes + shard + links
    slots = n_dom * width
    piece = (nodes + shard) // n_tm
    vmem = pl.BlockSpec(memory_space=pltpu.VMEM)
    smem = pl.BlockSpec(memory_space=pltpu.SMEM)
    specs = [vmem] * len(operands)
    specs[6] = smem
    specs[12] = smem
    state = pltpu.VMEM((total, samples), F32)
    tile = pltpu.VMEM((LANES, LANES), F32)
    return pl.pallas_call(
        functools.partial(kernel, cap, width, n_tm, n_dom),
        out_shape=(
            jax.ShapeDtypeStruct((nodes, samples), F32),
            jax.ShapeDtypeStruct((shared, samples), F32),
            jax.ShapeDtypeStruct((8, LANES), F32),
        ),
        in_specs=specs,
        out_specs=(vmem, vmem, vmem),
        scratch_shapes=[
            state,
            state,
            state,
            state,
            state,
            state,
            pltpu.VMEM((links, samples), F32),
            pltpu.VMEM((nblocks, bsize, 2 * samples), BF16),
            pltpu.VMEM((nblocks, bsize, 2 * samples), BF16),
            pltpu.VMEM((links, 2 * samples), BF16),
            pltpu.VMEM((slots, 2 * samples), BF16),
            pltpu.VMEM((nblocks, bsize, 4 * bsize), BF16),
            pltpu.VMEM((nodes, links), BF16),
            pltpu.VMEM((links, nodes), BF16),
            pltpu.VMEM((slots, links), BF16),
            pltpu.VMEM((links, slots), BF16),
            pltpu.VMEM((shard, slots), BF16),
            pltpu.VMEM((slots, shard), BF16),
            tile,
            tile,
            tile,
            pltpu.VMEM((links, samples), F32),
            pltpu.VMEM((links, samples), F32),
            pltpu.VMEM((shard, samples), F32),
            pltpu.VMEM((4, n_dom, width, samples), F32),
            pltpu.VMEM((4, n_dom, width, samples), F32),
            pltpu.VMEM((n_dom, 8, LANES), F32),
            pltpu.VMEM((n_dom, 8, LANES), F32),
            pltpu.VMEM((n_tm, 8, LANES), F32),
            pltpu.VMEM((n_tm, 8, LANES), F32),
            pltpu.VMEM((8, LANES), F32),
            pltpu.VMEM((n_dom, 8, LANES), F32),
            pltpu.VMEM((n_tm, piece, samples), F32),
            pltpu.VMEM((n_tm, piece, samples), F32),
            pltpu.VMEM((n_tm, piece, samples), F32),
            pltpu.VMEM((shard, samples), F32),
            pltpu.SemaphoreType.DMA((7, n_dom)),
            pltpu.SemaphoreType.DMA((7, n_dom)),
            pltpu.SemaphoreType.DMA((4, n_tm)),
            pltpu.SemaphoreType.DMA((4, n_tm)),
        ],
        compiler_params=pltpu.CompilerParams(
            collective_id=collective_id, has_side_effects=True, vmem_limit_bytes=62 * 1024 * 1024
        ),
        name="parareal",
    )(*operands)


def shards(
    state_interior,
    state_shared,
    gain_interior,
    gain_shared,
    jac_blocks,
    off_blocks,
    block_link,
    mass,
    shared_mass,
    shared_diag,
    link_node,
    link_shared,
    link_cond,
    source_amp,
    phase,
    nonlin,
):
    n_tm, n_dom = lax.axis_size("tm"), lax.axis_size("dom")

    def lanes(value):
        return value.reshape(-1, LANES)

    operands = (
        state_interior[0],
        state_shared[0],
        lanes(gain_interior),
        lanes(gain_shared),
        jac_blocks,
        off_blocks,
        block_link,
        lanes(mass),
        lanes(shared_mass),
        lanes(shared_diag),
        lanes(link_node),
        lanes(link_shared),
        lanes(link_shared),
        lanes(link_cond),
        source_amp,
        lanes(phase),
        lanes(nonlin),
    )
    shard = state_shared.shape[1] // n_dom
    new_in, new_sh, crowd = run(shard, shard, 0, n_tm, n_dom, operands)
    return (new_in[None], new_sh[None])


def solution(mesh):
    return jax.shard_map(
        shards,
        mesh=mesh,
        in_specs=(
            P("tm", "dom", None),
            P("tm", None, None),
            P("tm", "dom"),
            P("tm", None),
            P("dom", None, None),
            P("dom", None, None),
            P("dom"),
            P("dom"),
            P(),
            P(),
            P("dom"),
            P("dom"),
            P("dom"),
            P("dom", None),
            P("dom"),
            P(),
        ),
        out_specs=(P("tm", "dom", None), P("tm", None, None)),
        check_vma=False,
    )
```

```python
import functools
import math

import jax
import jax.numpy as jnp
from jax import lax
from jax.experimental import pallas as pl
from jax.experimental.pallas import tpu as pltpu
from jax.sharding import PartitionSpec as P

FINE = 2
NEWTON = 2
SHIFT = 8.0
SLOTS = 96
LANES = 128
MESH = pl.DeviceIdType.MESH
F32 = jnp.float32
BF16 = jnp.bfloat16

COL_MASS, COL_SIN, COL_GAIN, COL_SHARED, COL_NODE, COL_LINK, COL_COND = 0, 16, 48, 64, 72, 80, 88
FLOW_G, FLOW_P, BACK_P, BACK_Q, SETUP, GRAM, LAST = range(7)


def halves(acc):
    return acc[:, :LANES] + acc[:, LANES:]


def split(value):
    high = value.astype(BF16)
    low = (value - high.astype(F32)).astype(BF16)
    return jnp.concatenate([high, low], axis=1)


def dot(a, b):
    return jnp.dot(a, b, preferred_element_type=F32)


def ones_where(mask):
    return jnp.where(mask, 1.0, 0.0).astype(BF16)


def kernel(
    cap,
    width,
    n_tm,
    n_dom,
    x0_ref,
    w0_ref,
    gain_in_ref,
    gain_sh_ref,
    jac_ref,
    off_ref,
    block_link_ref,
    mass_ref,
    shared_mass_ref,
    shared_diag_ref,
    node_ref,
    link_ref,
    link_smem,
    cond_ref,
    amp_ref,
    phase_ref,
    nonlin_ref,
    out_in_ref,
    out_sh_ref,
    flag_ref,
    x,
    jx,
    g,
    p,
    q,
    fixed,
    flow,
    g_parts,
    p_parts,
    flow_parts,
    slot_parts,
    blocks,
    node_rows,
    node_cols,
    pack,
    unpack,
    own,
    own_t,
    table,
    table_t,
    table2_t,
    link_mass,
    link_cond,
    diag_sh,
    stage,
    recv,
    set_send,
    set_recv,
    gain_send,
    gain_recv,
    gram_send,
    gram_recv,
    jump_send,
    jump_recv,
    value_send,
    value_sh,
    send_sem,
    recv_sem,
    tm_send,
    tm_recv,
):
    me_t, me_d = lax.axis_index("tm"), lax.axis_index("dom")
    nodes = x0_ref.shape[0]
    shard = w0_ref.shape[0] // n_dom
    links = flow.shape[0]
    chunks, shard_chunks, link_chunks = nodes // LANES, shard // LANES, links // LANES
    at_sh, at_link = nodes, nodes + shard
    per_owner = width // LANES
    nblocks, bsize = jac_ref.shape[0], jac_ref.shape[1]
    iota0 = lax.broadcasted_iota(jnp.int32, (LANES, LANES), 0)
    iota1 = lax.broadcasted_iota(jnp.int32, (LANES, LANES), 1)

    def rows(start, size):
        return pl.ds(pl.multiple_of(start, size), size)

    def dom_peer(step):
        return lax.rem(me_d + step, n_dom)

    def dom_source(step):
        return lax.rem(me_d + n_dom - step, n_dom)

    def tm_peer(step):
        return lax.rem(me_t + step, n_tm)

    def tm_source(step):
        return lax.rem(me_t + n_tm - step, n_tm)

    def dom_copy(kind, step, source, target):
        return pltpu.make_async_remote_copy(
            src_ref=source,
            dst_ref=target,
            send_sem=send_sem.at[kind, step],
            recv_sem=recv_sem.at[kind, step],
            device_id={"dom": dom_peer(step)},
            device_id_type=MESH,
        )

    def tm_copy(kind, step, source, target):
        return pltpu.make_async_remote_copy(
            src_ref=source,
            dst_ref=target,
            send_sem=tm_send.at[kind, step],
            recv_sem=tm_recv.at[kind, step],
            device_id={"tm": tm_peer(step)},
            device_id_type=MESH,
        )

    if cap < width:
        for kind in range(4):
            for o in range(n_dom):
                recv[kind, o, cap:, :] = jnp.zeros((width - cap, LANES), F32)
    barrier = pltpu.get_barrier_semaphore()
    for step in range(1, n_dom):
        pl.semaphore_signal(barrier, inc=1, device_id={"dom": dom_peer(step)}, device_id_type=MESH)
    for step in range(1, n_tm):
        pl.semaphore_signal(barrier, inc=1, device_id={"tm": tm_peer(step)}, device_id_type=MESH)

    slice_f = me_t.astype(F32)
    table[...] = jnp.zeros((LANES, LANES), F32)
    table[COL_MASS : COL_MASS + chunks, :] = mass_ref[...]
    for k in range(FINE):
        angle = (slice_f * FINE + (k + 1.0)) * (2.0 * math.pi / (n_tm * FINE))
        at = COL_SIN + chunks * k
        table[at : at + chunks, :] = jnp.sin(angle + phase_ref[...])
    table[COL_GAIN : COL_GAIN + chunks, :] = gain_in_ref[...]
    for a in range(shard_chunks):
        row = shard_chunks * me_d + a
        table[COL_SHARED + a : COL_SHARED + a + 1, :] = shared_mass_ref[pl.ds(row, 1), :]
        table[COL_SHARED + 2 + a : COL_SHARED + 3 + a, :] = shared_diag_ref[pl.ds(row, 1), :]
        table[COL_SHARED + 4 + a : COL_SHARED + 5 + a, :] = gain_sh_ref[pl.ds(row, 1), :]
    table[COL_NODE : COL_NODE + link_chunks, :] = node_ref[...].astype(F32)
    table[COL_LINK : COL_LINK + link_chunks, :] = link_ref[...].astype(F32)
    table[COL_COND : COL_COND + link_chunks, :] = cond_ref[...]
    table_t[...] = table[...].T

    def column(at):
        return table_t[:, at : at + 1]

    link_col = [column(COL_LINK + j).astype(jnp.int32) for j in range(link_chunks)]
    link_row = [link_ref[j : j + 1, :] for j in range(link_chunks)]
    if cap == width:
        slot_col, slot_row = link_col, link_row
        crowd = jnp.zeros((1, LANES), F32)
    else:
        owner_col = [v // shard for v in link_col]
        owner_row = [v // shard for v in link_row]
        slot_col, slot_row = [], []
        crowd = jnp.zeros((1, LANES), F32)
        for j in range(link_chunks):
            rank_row = jnp.zeros((1, LANES), F32)
            rank_col = jnp.zeros((LANES, 1), F32)
            for i in range(j + 1):
                same_row = owner_col[i] == owner_row[j]
                same_col = owner_col[j] == owner_row[i]
                if i == j:
                    same_row = same_row & (iota0 < iota1)
                    same_col = same_col & (iota1 < iota0)
                rank_row += jnp.sum(jnp.where(same_row, 1.0, 0.0), axis=0, keepdims=True)
                rank_col += jnp.sum(jnp.where(same_col, 1.0, 0.0), axis=1, keepdims=True)
            crowd = jnp.maximum(crowd, rank_row)
            slot_row.append(owner_row[j] * width + rank_row.astype(jnp.int32))
            slot_col.append(owner_col[j] * width + rank_col.astype(jnp.int32))
    set_send[...] = jnp.zeros(set_send.shape, F32)
    for i in range(n_dom * per_owner):
        held = jnp.full((1, LANES), -1.0, F32)
        total = jnp.zeros((1, LANES), F32)
        for j in range(link_chunks):
            here = (iota1 + LANES * i) == slot_col[j]
            local = (link_col[j] % shard).astype(F32)
            held = jnp.maximum(held, jnp.max(jnp.where(here, local, -1.0), axis=0, keepdims=True))
            total += jnp.sum(jnp.where(here, column(COL_COND + j), 0.0), axis=0, keepdims=True)
            unpack[LANES * j : LANES * (j + 1), LANES * i : LANES * (i + 1)] = ones_where(here)
            pack[LANES * i : LANES * (i + 1), LANES * j : LANES * (j + 1)] = ones_where(
                (iota0 + LANES * i) == slot_row[j]
            )
        o, h = i // per_owner, i % per_owner
        set_send[o, h : h + 1, :] = held
        set_send[o, 2 + h : 3 + h, :] = total
    for o in range(n_dom):
        set_send[o, 4:5, :] = crowd
    gain_send[...] = jnp.zeros(gain_send.shape, F32)
    for m in range(n_tm):
        gain_send[m, 0:1, :] = gain_in_ref[m : m + 1, :]
        row = shard_chunks * me_d + m * shard_chunks // n_tm
        gain_send[m, 1:2, :] = gain_sh_ref[pl.ds(row, 1), :]

    pl.semaphore_wait(barrier, n_dom - 1 + n_tm - 1)
    for step in range(1, n_dom):
        dom_copy(SETUP, step, set_send.at[dom_peer(step)], set_recv.at[me_d]).start()
    for step in range(1, n_tm):
        tm_copy(0, step, gain_send.at[tm_peer(step)], gain_recv.at[me_t]).start()
    set_recv[me_d] = set_send[me_d]
    gain_recv[me_t] = gain_send[me_t]

    for j in range(link_chunks):
        node_row = node_ref[j : j + 1, :]
        node_col = column(COL_NODE + j).astype(jnp.int32)
        link_cond[LANES * j : LANES * (j + 1), :] = jnp.broadcast_to(column(COL_COND + j), (LANES, LANES))
        across = slice(LANES * j, LANES * (j + 1))

        def select(i, carry):
            base = pl.multiple_of(i * LANES, LANES)
            node_rows[pl.ds(base, LANES), across] = ones_where(iota0 + base == node_row)
            node_cols[across, pl.ds(base, LANES)] = ones_where(iota1 + base == node_col)
            return carry

        lax.fori_loop(0, chunks, select, 0, unroll=2)
        mass_sum = jnp.zeros((LANES, LANES), F32)
        for i in range(w0_ref.shape[0] // LANES):
            mass_sum += jnp.where(iota1 + LANES * i == link_col[j], shared_mass_ref[i : i + 1, :], 0.0)
        link_mass[across, :] = jnp.broadcast_to(jnp.sum(mass_sum, axis=1, keepdims=True), (LANES, LANES))

    def cut(b, carry):
        blocks[b] = split(jnp.concatenate([jac_ref[b], off_ref[b]], axis=1))
        return carry

    lax.fori_loop(0, nblocks, cut, 0, unroll=2)

    each = LANES // bsize

    def begin(i, carry):
        at = rows(i * LANES, LANES)
        value = x0_ref[at, :]
        x[at, :] = value
        g_parts[pl.ds(i * each, each)] = split(value).reshape(each, bsize, 2 * LANES)
        return carry

    lax.fori_loop(0, chunks, begin, 0)
    x[at_sh : at_sh + shard, :] = w0_ref[rows(me_d * shard, shard), :]

    def fetch(l, carry):
        x[pl.ds(at_link + l, 1), :] = w0_ref[pl.ds(link_smem[l // LANES, lax.rem(l, LANES)], 1), :]
        return carry

    lax.fori_loop(0, links, fetch, 0, unroll=8)

    for step in range(1, n_dom):
        dom_copy(SETUP, step, set_send.at[dom_peer(step)], set_recv.at[dom_source(step)]).wait_recv()
    for o in range(n_dom):
        for h in range(per_owner):
            at = o * per_owner + h
            table[at : at + 1, :] = set_recv[o, h : h + 1, :]
    table2_t[...] = table[...].T
    sums = [jnp.zeros((LANES, LANES), F32) for a in range(shard_chunks)]
    crowd = jnp.zeros((1, LANES), F32)
    for o in range(n_dom):
        crowd = jnp.maximum(crowd, set_recv[o, 4:5, :])
        for h in range(per_owner):
            i = o * per_owner + h
            held_row = set_recv[o, h : h + 1, :].astype(jnp.int32)
            held_col = table2_t[:, i : i + 1].astype(jnp.int32)
            for a in range(shard_chunks):
                here = (iota0 + LANES * a) == held_row
                sums[a] += jnp.where(here, set_recv[o, 2 + h : 3 + h, :], 0.0)
                own[LANES * a : LANES * (a + 1), LANES * i : LANES * (i + 1)] = ones_where(here)
                own_t[LANES * i : LANES * (i + 1), LANES * a : LANES * (a + 1)] = ones_where(
                    (iota1 + LANES * a) == held_col
                )
    for a in range(shard_chunks):
        total = column(COL_SHARED + 2 + a) + jnp.sum(sums[a], axis=1, keepdims=True)
        diag_sh[LANES * a : LANES * (a + 1), :] = jnp.broadcast_to(total, (LANES, LANES))
    flag_ref[...] = jnp.broadcast_to(crowd, flag_ref.shape)

    def apply_blocks(parts, out):
        def one(b, carry):
            other = block_link_ref[b]
            mine, theirs = parts[b], parts[other]
            acc = dot(blocks[b], jnp.concatenate([mine, theirs, mine, theirs], axis=0))
            out[rows(b * bsize, bsize), :] = halves(acc)
            return carry

        lax.fori_loop(0, nblocks, one, 0, unroll=4)

    def gather_flow(parts):
        flow[...] = halves(dot(node_cols[...], parts[...].reshape(nodes, 2 * LANES))) * link_cond[...]

    def add_flow(vec, out, shift_by=None, parts=None):
        flow_parts[...] = split(flow[...] - link_cond[...] * vec[at_link : at_link + links, :])
        size = 2 * LANES

        def one(i, carry):
            at = rows(i * size, size)
            value = out[at, :] + halves(dot(node_rows[at, :], flow_parts[...]))
            if shift_by is not None:
                value = value - SHIFT * shift_by[at, :]
            out[at, :] = value
            if parts is not None:
                parts[pl.ds(i * 2 * each, 2 * each)] = split(value).reshape(2 * each, bsize, 2 * LANES)
            return carry

        lax.fori_loop(0, nodes // size, one, 0)

    def start_exchange(kind):
        for step in range(1, n_dom):
            dom_copy(
                kind,
                step,
                stage.at[kind, dom_peer(step), pl.ds(0, cap)],
                recv.at[kind, me_d, pl.ds(0, cap)],
            ).start()
        recv[kind, me_d] = stage[kind, me_d]

    def wait_exchange(kind, receive):
        for step in range(1, n_dom):
            copy = dom_copy(
                kind,
                step,
                stage.at[kind, dom_peer(step), pl.ds(0, cap)],
                recv.at[kind, dom_source(step), pl.ds(0, cap)],
            )
            if receive:
                copy.wait_recv()
            else:
                copy.wait_send()

    def send_flow(kind):
        flow_parts[...] = split(flow[...])

        def one(o, carry):
            stage[kind, o] = halves(dot(pack[rows(o * width, width), :], flow_parts[...]))
            return carry

        lax.fori_loop(0, n_dom, one, 0)
        start_exchange(kind)

    def load_slots(kind):
        for o in range(n_dom):
            slot_parts[o * width : (o + 1) * width, :] = split(recv[kind, o])

    def collect_flow(kind):
        wait_exchange(kind, True)
        load_slots(kind)
        return halves(dot(own[...], slot_parts[...]))

    def send_back(kind, value):
        value_parts = split(value)

        def one(o, carry):
            stage[kind, o] = halves(dot(own_t[rows(o * width, width), :], value_parts))
            return carry

        lax.fori_loop(0, n_dom, one, 0)
        start_exchange(kind)

    def take_back(kind, out):
        wait_exchange(kind, True)
        load_slots(kind)
        out[at_link : at_link + links, :] = halves(dot(unpack[...], slot_parts[...]))

    def set_fixed(k):
        for i in range(chunks):
            at = slice(LANES * i, LANES * (i + 1))
            drive = amp_ref[at, :] * column(COL_SIN + chunks * k + i)
            fixed[at, :] = column(COL_MASS + i) * x[at, :] + drive
        for a in range(shard_chunks):
            at = slice(at_sh + LANES * a, at_sh + LANES * (a + 1))
            fixed[at, :] = column(COL_SHARED + a) * x[at, :]
        fixed[at_link:, :] = link_mass[...] * x[at_link:, :]

    def new_residual():
        def one(i, carry):
            at = rows(i * LANES, LANES)
            value = fixed[at, :] - jx[at, :] - nonlin_ref[...] * jnp.tanh(x[at, :])
            g[at, :] = value
            g_parts[pl.ds(i * each, each)] = split(value).reshape(each, bsize, 2 * LANES)
            return carry

        lax.fori_loop(0, chunks, one, 0)
        g[nodes:, :] = fixed[nodes:, :] - jx[nodes:, :]

    gather_flow(g_parts)
    send_flow(FLOW_G)
    apply_blocks(g_parts, jx)
    add_flow(x, jx)
    set_fixed(0)
    at = slice(at_sh, at_sh + shard)
    wait_exchange(FLOW_G, False)
    jx[at, :] = diag_sh[...] * x[at, :] - collect_flow(FLOW_G)
    send_back(BACK_P, jx[at, :])
    take_back(BACK_P, jx)
    wait_exchange(BACK_P, False)
    new_residual()

    def gram_row(index, total):
        return total[index : index + 1, :]

    def newton(turn, carry):
        gather_flow(g_parts)
        send_flow(FLOW_G)
        apply_blocks(g_parts, p)
        add_flow(g, p, g, p_parts)
        gather_flow(p_parts)
        send_flow(FLOW_P)
        apply_blocks(p_parts, q)
        p[at, :] = (diag_sh[...] - SHIFT) * g[at, :] - collect_flow(FLOW_G)
        send_back(BACK_P, p[at, :])
        q[at, :] = diag_sh[...] * p[at, :] - collect_flow(FLOW_P)
        send_back(BACK_Q, q[at, :])
        take_back(BACK_P, p)
        add_flow(p, q)

        def gram(i, sums):
            here = rows(i * LANES, LANES)
            vg, vp, vq = g[here, :], p[here, :], q[here, :]
            pairs = ((vg, vg), (vg, vp), (vp, vp), (vg, vq), (vp, vq), (vq, vq))
            return tuple(
                s + jnp.sum((a * b).reshape(LANES // 8, 8, LANES), axis=0)
                for s, (a, b) in zip(sums, pairs)
            )

        zero = jnp.zeros((8, LANES), F32)
        sums = lax.fori_loop(0, chunks + shard_chunks, gram, (zero,) * 6)
        for i, s in enumerate(sums):
            gram_send[i : i + 1, :] = jnp.sum(s, axis=0, keepdims=True)
        gram_send[6:8, :] = jnp.zeros((2, LANES), F32)
        for step in range(1, n_dom):
            dom_copy(GRAM, step, gram_send, gram_recv.at[me_d]).start()
        gram_recv[me_d] = gram_send[...]
        for kind in (FLOW_G, FLOW_P, BACK_P, BACK_Q):
            wait_exchange(kind, False)
        for step in range(1, n_dom):
            copy = dom_copy(GRAM, step, gram_send, gram_recv.at[dom_source(step)])
            copy.wait_send()
            copy.wait_recv()
        total = gram_recv[0]
        for o in range(1, n_dom):
            total = total + gram_recv[o]
        gg, gp, pp, gq, pq, qq = [total[i : i + 1, :] for i in range(6)]
        norm2 = gg + 1e-30
        inv2 = 1.0 / norm2
        h00 = (gp + SHIFT * gg) * inv2
        turnover = h00 - SHIFT
        tail2 = pp - 2.0 * turnover * gp + turnover * turnover * gg
        inv_both = 1.0 / (jnp.sqrt(norm2) * jnp.sqrt(tail2))
        inv_tail2 = 1.0 / tail2
        push = turnover * SHIFT
        g_s = gq - turnover * gp - push * gg
        p_s = pq - turnover * pp - push * gp
        q_s = qq - turnover * pq - push * gq
        t_s = p_s - turnover * g_s
        s_s = q_s - turnover * p_s - push * g_s
        g_t = gp - turnover * gg
        h10 = tail2 * inv_both
        h01 = g_s * inv_both
        h11 = t_s * inv_tail2
        h21_2 = (
            s_s * inv_tail2
            - h01 * h01 * (2.0 - gg * inv2)
            - h11 * h11
            + 2.0 * h01 * h11 * g_t * inv_both
        )
        n11 = h00 * h00 + h10 * h10
        n12 = h00 * h01 + h10 * h11
        n22 = h01 * h01 + h11 * h11 + h21_2
        inv_det = 1.0 / (n11 * n22 - n12 * n12)
        c_p = norm2 * inv_both * (h01 * n11 - h00 * n12) * inv_det
        c_g = (h00 * n22 - h01 * n12) * inv_det - turnover * c_p

        def advance(here):
            vg, vp = g[here, :], p[here, :]
            x[here, :] = x[here, :] + c_g * vg + c_p * vp
            jx[here, :] = jx[here, :] + c_g * (vp + SHIFT * vg) + c_p * q[here, :]

        def one(i, carry):
            advance(rows(i * LANES, LANES))
            return carry

        lax.fori_loop(0, chunks + shard_chunks, one, 0)
        take_back(BACK_Q, q)
        advance(slice(at_link, at_link + links))

        @pl.when(turn == NEWTON - 1)
        def _():
            set_fixed(1)

        @pl.when(turn < FINE * NEWTON - 1)
        def _():
            new_residual()

        return carry

    lax.fori_loop(0, FINE * NEWTON, newton, 0)

    per_rows, per_shared = nodes // n_tm, shard // n_tm
    for i in range(chunks):
        here = slice(LANES * i, LANES * (i + 1))
        jump_send[i, :per_rows, :] = x[here, :] - column(COL_GAIN + i) * x0_ref[here, :]
    for a in range(shard_chunks):
        here = slice(at_sh + LANES * a, at_sh + LANES * (a + 1))
        start = w0_ref[rows(me_d * shard + LANES * a, LANES), :]
        jump = x[here, :] - column(COL_SHARED + 4 + a) * start
        pieces = LANES // per_shared
        for m in range(pieces):
            jump_send[a * pieces + m, per_rows:, :] = jump[per_shared * m : per_shared * (m + 1), :]
    for step in range(1, n_tm):
        tm_copy(1, step, jump_send.at[tm_peer(step)], jump_recv.at[me_t]).start()
    jump_recv[me_t] = jump_send[me_t]
    for step in range(1, n_tm):
        tm_copy(0, step, gain_send.at[tm_peer(step)], gain_recv.at[tm_source(step)]).wait_recv()
    for m in range(n_tm):
        table[m : m + 1, :] = gain_recv[m, 0:1, :]
        table[n_tm + m : n_tm + m + 1, :] = gain_recv[m, 1:2, :]
    table2_t[...] = table[...].T
    my_shared = rows(lax.rem(me_t, LANES // per_shared) * per_shared, per_shared)
    for step in range(1, n_tm):
        tm_copy(1, step, jump_send.at[tm_peer(step)], jump_recv.at[tm_source(step)]).wait_recv()
    for part, gains in (
        (slice(0, per_rows), [table2_t[:, m : m + 1] for m in range(n_tm)]),
        (
            slice(per_rows, per_rows + per_shared),
            [table2_t[my_shared, n_tm + m : n_tm + m + 1] for m in range(n_tm)],
        ),
    ):
        whole, total = gains[0], jump_recv[0, part, :]
        for m in range(1, n_tm):
            whole = whole * gains[m]
            total = gains[m] * total + jump_recv[m, part, :]
        value = total / (1.0 - whole)
        for m in range(n_tm):
            value_send[m, part, :] = value
            if m + 1 < n_tm:
                value = gains[m] * value + jump_recv[m, part, :]

    def value_copy(step, holder):
        source = value_send.at[tm_peer(step), pl.ds(0, per_rows)]
        return tm_copy(2, step, source, out_in_ref.at[rows(holder * per_rows, per_rows)])

    def shared_copy(step, holder):
        source = value_send.at[tm_peer(step), pl.ds(per_rows, per_shared)]
        return tm_copy(3, step, source, value_sh.at[rows(holder * per_shared, per_shared)])

    for step in range(1, n_tm):
        shared_copy(step, me_t).start()
        value_copy(step, me_t).start()
    out_in_ref[rows(me_t * per_rows, per_rows), :] = value_send[me_t, :per_rows, :]
    value_sh[rows(me_t * per_shared, per_shared), :] = value_send[me_t, per_rows:, :]
    for step in range(1, n_tm):
        shared_copy(step, tm_source(step)).wait_recv()
    for step in range(1, n_dom):
        dom_copy(LAST, step, value_sh, out_sh_ref.at[rows(me_d * shard, shard)]).start()
    out_sh_ref[rows(me_d * shard, shard), :] = value_sh[...]
    for step in range(1, n_tm):
        value_copy(step, tm_source(step)).wait_recv()
    for step in range(1, n_dom):
        copy = dom_copy(LAST, step, value_sh, out_sh_ref.at[rows(dom_source(step) * shard, shard)])
        copy.wait_recv()
        copy.wait_send()
        dom_copy(SETUP, step, set_send.at[dom_peer(step)], set_recv.at[me_d]).wait_send()
    for step in range(1, n_tm):
        tm_copy(0, step, gain_send.at[tm_peer(step)], gain_recv.at[me_t]).wait_send()
        tm_copy(1, step, jump_send.at[tm_peer(step)], jump_recv.at[me_t]).wait_send()
        shared_copy(step, me_t).wait_send()
        value_copy(step, me_t).wait_send()


def run(cap, width, collective_id, n_tm, n_dom, operands):
    nodes, samples = operands[0].shape
    shared = operands[1].shape[0]
    shard = shared // n_dom
    links = operands[10].shape[0] * operands[10].shape[1]
    nblocks, bsize = operands[4].shape[0], operands[4].shape[1]
    total = nodes + shard + links
    slots = n_dom * width
    piece = (nodes + shard) // n_tm
    vmem = pl.BlockSpec(memory_space=pltpu.VMEM)
    smem = pl.BlockSpec(memory_space=pltpu.SMEM)
    specs = [vmem] * len(operands)
    specs[6] = smem
    specs[12] = smem
    state = pltpu.VMEM((total, samples), F32)
    tile = pltpu.VMEM((LANES, LANES), F32)
    return pl.pallas_call(
        functools.partial(kernel, cap, width, n_tm, n_dom),
        out_shape=(
            jax.ShapeDtypeStruct((nodes, samples), F32),
            jax.ShapeDtypeStruct((shared, samples), F32),
            jax.ShapeDtypeStruct((8, LANES), F32),
        ),
        in_specs=specs,
        out_specs=(vmem, vmem, vmem),
        scratch_shapes=[
            state,
            state,
            state,
            state,
            state,
            state,
            pltpu.VMEM((links, samples), F32),
            pltpu.VMEM((nblocks, bsize, 2 * samples), BF16),
            pltpu.VMEM((nblocks, bsize, 2 * samples), BF16),
            pltpu.VMEM((links, 2 * samples), BF16),
            pltpu.VMEM((slots, 2 * samples), BF16),
            pltpu.VMEM((nblocks, bsize, 4 * bsize), BF16),
            pltpu.VMEM((nodes, links), BF16),
            pltpu.VMEM((links, nodes), BF16),
            pltpu.VMEM((slots, links), BF16),
            pltpu.VMEM((links, slots), BF16),
            pltpu.VMEM((shard, slots), BF16),
            pltpu.VMEM((slots, shard), BF16),
            tile,
            tile,
            tile,
            pltpu.VMEM((links, samples), F32),
            pltpu.VMEM((links, samples), F32),
            pltpu.VMEM((shard, samples), F32),
            pltpu.VMEM((4, n_dom, width, samples), F32),
            pltpu.VMEM((4, n_dom, width, samples), F32),
            pltpu.VMEM((n_dom, 8, LANES), F32),
            pltpu.VMEM((n_dom, 8, LANES), F32),
            pltpu.VMEM((n_tm, 8, LANES), F32),
            pltpu.VMEM((n_tm, 8, LANES), F32),
            pltpu.VMEM((8, LANES), F32),
            pltpu.VMEM((n_dom, 8, LANES), F32),
            pltpu.VMEM((n_tm, piece, samples), F32),
            pltpu.VMEM((n_tm, piece, samples), F32),
            pltpu.VMEM((n_tm, piece, samples), F32),
            pltpu.VMEM((shard, samples), F32),
            pltpu.SemaphoreType.DMA((7, n_dom)),
            pltpu.SemaphoreType.DMA((7, n_dom)),
            pltpu.SemaphoreType.DMA((4, n_tm)),
            pltpu.SemaphoreType.DMA((4, n_tm)),
        ],
        compiler_params=pltpu.CompilerParams(
            collective_id=collective_id, has_side_effects=True, vmem_limit_bytes=62 * 1024 * 1024
        ),
        name="parareal",
    )(*operands)


def shards(
    state_interior,
    state_shared,
    gain_interior,
    gain_shared,
    jac_blocks,
    off_blocks,
    block_link,
    mass,
    shared_mass,
    shared_diag,
    link_node,
    link_shared,
    link_cond,
    source_amp,
    phase,
    nonlin,
):
    n_tm, n_dom = lax.axis_size("tm"), lax.axis_size("dom")

    def lanes(value):
        return value.reshape(-1, LANES)

    operands = (
        state_interior[0],
        state_shared[0],
        lanes(gain_interior),
        lanes(gain_shared),
        jac_blocks,
        off_blocks,
        block_link,
        lanes(mass),
        lanes(shared_mass),
        lanes(shared_diag),
        lanes(link_node),
        lanes(link_shared),
        lanes(link_shared),
        lanes(link_cond),
        source_amp,
        lanes(phase),
        lanes(nonlin),
    )
    shard = state_shared.shape[1] // n_dom
    new_in, new_sh, crowd = run(SLOTS, LANES, 0, n_tm, n_dom, operands)
    new_in, new_sh = lax.cond(
        jnp.max(crowd) < SLOTS,
        lambda: (new_in, new_sh),
        lambda: run(shard, shard, 1, n_tm, n_dom, operands)[:2],
    )
    return (new_in[None], new_sh[None])


def solution(mesh):
    return jax.shard_map(
        shards,
        mesh=mesh,
        in_specs=(
            P("tm", "dom", None),
            P("tm", None, None),
            P("tm", "dom"),
            P("tm", None),
            P("dom", None, None),
            P("dom", None, None),
            P("dom"),
            P("dom"),
            P(),
            P(),
            P("dom"),
            P("dom"),
            P("dom"),
            P("dom", None),
            P("dom"),
            P(),
        ),
        out_specs=(P("tm", "dom", None), P("tm", None, None)),
        check_vma=False,
    )
```

```python
import functools
import math

import jax
import jax.numpy as jnp
from jax import lax
from jax.experimental import pallas as pl
from jax.experimental.pallas import tpu as pltpu
from jax.sharding import PartitionSpec as P

FINE = 2
NEWTON = 2
SHIFT = 8.0
SLOTS = 96
LANES = 128
MESH = pl.DeviceIdType.MESH
F32 = jnp.float32
BF16 = jnp.bfloat16

COL_MASS, COL_SIN, COL_GAIN, COL_SHARED, COL_NODE, COL_LINK, COL_COND = 0, 16, 48, 64, 72, 80, 88
ABSENT = 2.0**20
FLOW_G, FLOW_P, BACK_P, BACK_Q, SETUP, GRAM, LAST = range(7)


def halves(acc):
    return acc[:, :LANES] + acc[:, LANES:]


def split(value):
    high = value.astype(BF16)
    low = (value - high.astype(F32)).astype(BF16)
    return jnp.concatenate([high, low], axis=1)


def dot(a, b):
    return jnp.dot(a, b, preferred_element_type=F32)


def ones_where(mask):
    return jnp.where(mask, 1.0, 0.0).astype(BF16)


def kernel(
    cap,
    width,
    bucket_nodes,
    bucket_cap,
    n_tm,
    n_dom,
    x0_ref,
    w0_ref,
    gain_in_ref,
    gain_sh_ref,
    jac_ref,
    off_ref,
    block_link_ref,
    mass_ref,
    shared_mass_ref,
    shared_diag_ref,
    node_ref,
    link_ref,
    cond_ref,
    amp_ref,
    phase_ref,
    nonlin_ref,
    out_in_ref,
    out_sh_ref,
    flag_ref,
    x,
    jx,
    g,
    p,
    q,
    fixed,
    g_parts,
    p_parts,
    flow_parts,
    slot_parts,
    blocks,
    node_cols,
    bucket_rows,
    scatter_parts,
    shared_cols,
    pack,
    unpack,
    own,
    own_t,
    table,
    table_t,
    table2_t,
    link_mass,
    link_cond,
    diag_sh,
    stage,
    recv,
    set_send,
    set_recv,
    gain_send,
    gain_recv,
    gram_send,
    gram_recv,
    jump_send,
    jump_recv,
    value_send,
    jump_sh_send,
    jump_sh_recv,
    value_sh_send,
    pair_gain,
    pair_jump,
    pair_value,
    value_recv,
    value_sh,
    send_sem,
    recv_sem,
    tm_send,
    tm_recv,
):
    me_t, me_d = lax.axis_index("tm"), lax.axis_index("dom")
    nodes = x0_ref.shape[0]
    shard = w0_ref.shape[0] // n_dom
    links = flow_parts.shape[0]
    chunks, shard_chunks, link_chunks = nodes // LANES, shard // LANES, links // LANES
    at_sh, at_link = nodes, nodes + shard
    per_owner = width // LANES
    nblocks, bsize = jac_ref.shape[0], jac_ref.shape[1]
    iota0 = lax.broadcasted_iota(jnp.int32, (LANES, LANES), 0)
    iota1 = lax.broadcasted_iota(jnp.int32, (LANES, LANES), 1)

    def rows(start, size):
        return pl.ds(pl.multiple_of(start, size), size)

    def dom_peer(step):
        return lax.rem(me_d + step, n_dom)

    def dom_source(step):
        return lax.rem(me_d + n_dom - step, n_dom)

    def tm_peer(step):
        return lax.rem(me_t + step, n_tm)

    def tm_source(step):
        return lax.rem(me_t + n_tm - step, n_tm)

    def dom_copy(kind, step, source, target):
        return pltpu.make_async_remote_copy(
            src_ref=source,
            dst_ref=target,
            send_sem=send_sem.at[kind, step],
            recv_sem=recv_sem.at[kind, step],
            device_id={"dom": dom_peer(step)},
            device_id_type=MESH,
        )

    def tm_copy(kind, step, source, target):
        return pltpu.make_async_remote_copy(
            src_ref=source,
            dst_ref=target,
            send_sem=tm_send.at[kind, step],
            recv_sem=tm_recv.at[kind, step],
            device_id={"tm": tm_peer(step)},
            device_id_type=MESH,
        )

    pairs = n_tm // 2
    core, chip = lax.rem(me_t, 2), me_t // 2

    def pair_copy(kind, source, target):
        return pltpu.make_async_remote_copy(
            src_ref=source,
            dst_ref=target,
            send_sem=tm_send.at[4 + kind, 0],
            recv_sem=tm_recv.at[4 + kind, 0],
            device_id={"tm": me_t + 1 - 2 * core},
            device_id_type=MESH,
        )

    def chip_peer(step):
        return lax.rem(chip + step, pairs)

    def chip_source(step):
        return lax.rem(chip + pairs - step, pairs)

    def chip_copy(kind, step, source, target):
        return pltpu.make_async_remote_copy(
            src_ref=source,
            dst_ref=target,
            send_sem=tm_send.at[kind, step],
            recv_sem=tm_recv.at[kind, step],
            device_id={"tm": 2 * chip_peer(step) + core},
            device_id_type=MESH,
        )

    if cap < width:
        for kind in range(4):
            for o in range(n_dom):
                recv[kind, o, cap:, :] = jnp.zeros((width - cap, LANES), F32)
    barrier = pltpu.get_barrier_semaphore()
    for step in range(1, n_dom):
        pl.semaphore_signal(barrier, inc=1, device_id={"dom": dom_peer(step)}, device_id_type=MESH)
    for step in range(1, n_tm):
        pl.semaphore_signal(barrier, inc=1, device_id={"tm": tm_peer(step)}, device_id_type=MESH)

    slice_f = me_t.astype(F32)
    table[...] = jnp.zeros((LANES, LANES), F32)
    table[COL_MASS : COL_MASS + chunks, :] = mass_ref[...]
    for k in range(FINE):
        angle = (slice_f * FINE + (k + 1.0)) * (2.0 * math.pi / (n_tm * FINE))
        at = COL_SIN + chunks * k
        table[at : at + chunks, :] = jnp.sin(angle + phase_ref[...])
    table[COL_GAIN : COL_GAIN + chunks, :] = gain_in_ref[...]
    for a in range(shard_chunks):
        row = shard_chunks * me_d + a
        table[COL_SHARED + a : COL_SHARED + a + 1, :] = shared_mass_ref[pl.ds(row, 1), :]
        table[COL_SHARED + 2 + a : COL_SHARED + 3 + a, :] = shared_diag_ref[pl.ds(row, 1), :]
        table[COL_SHARED + 4 + a : COL_SHARED + 5 + a, :] = gain_sh_ref[pl.ds(row, 1), :]
    given = node_ref.shape[0]
    table[COL_NODE : COL_NODE + given, :] = node_ref[...].astype(F32)
    table[COL_LINK : COL_LINK + given, :] = link_ref[...].astype(F32)
    table[COL_COND : COL_COND + given, :] = cond_ref[...]
    table_t[...] = table[...].T

    def column(at):
        return table_t[:, at : at + 1]

    nbuckets = nodes // bucket_nodes
    bucket_rows[...] = jnp.zeros(bucket_rows.shape, F32)
    crowd = jnp.zeros((1, 1), F32)
    if nbuckets == 1:
        for j in range(given):
            across = slice(LANES * j, LANES * (j + 1))
            bucket_rows[0, 0:1, across] = node_ref[j : j + 1, :].astype(F32)
            bucket_rows[0, 1:2, across] = cond_ref[j : j + 1, :]
        table[0:given, :] = node_ref[...].astype(F32)
        table[8 : 8 + given, :] = link_ref[...].astype(F32)
        table[16 : 16 + given, :] = cond_ref[...]
    else:
        given_node = [column(COL_NODE + j) for j in range(given)]
        given_link = [column(COL_LINK + j) for j in range(given)]
        given_cond = [column(COL_COND + j) for j in range(given)]
        bucket_col = [v.astype(jnp.int32) // bucket_nodes for v in given_node]
        bucket_row = [node_ref[j : j + 1, :] // bucket_nodes for j in range(given)]
        place = []
        for j in range(given):
            rank = jnp.zeros((LANES, 1), F32)
            for i in range(j + 1):
                same = bucket_col[j] == bucket_row[i]
                if i == j:
                    same = same & (iota1 < iota0)
                rank += jnp.sum(jnp.where(same, 1.0, 0.0), axis=1, keepdims=True)
            crowd = jnp.maximum(crowd, jnp.max(rank, axis=0, keepdims=True))
            place.append((bucket_col[j], rank.astype(jnp.int32)))

        def picked(masks, values, none):
            total = jnp.zeros((1, LANES), F32)
            for mask, value in zip(masks, values):
                total += jnp.sum(jnp.where(mask, value + none, 0.0), axis=0, keepdims=True)
            return total - none

        for i in range(nbuckets):
            masks = [(b == i) & (iota1 == r) for b, r in place]
            bucket_rows[i, 0:1, :] = picked(masks, given_node, ABSENT)
            bucket_rows[i, 1:2, :] = picked(masks, given_cond, 0.0)
        for i in range(link_chunks):
            masks = [(iota1 + LANES * i) == b * bucket_cap + r for b, r in place]
            table[i : i + 1, :] = picked(masks, given_node, ABSENT)
            table[8 + i : 9 + i, :] = picked(masks, given_link, ABSENT)
            table[16 + i : 17 + i, :] = picked(masks, given_cond, 0.0)
    table2_t[...] = table[...].T

    link_col = [table2_t[:, 8 + j : 9 + j].astype(jnp.int32) for j in range(link_chunks)]
    link_row = [table[8 + j : 9 + j, :].astype(jnp.int32) for j in range(link_chunks)]
    if cap == width:
        slot_col, slot_row = link_col, link_row
    else:
        owner_col = [v // shard for v in link_col]
        owner_row = [v // shard for v in link_row]
        slot_col, slot_row = [], []
        for j in range(link_chunks):
            rank_row = jnp.zeros((1, LANES), F32)
            rank_col = jnp.zeros((LANES, 1), F32)
            for i in range(j + 1):
                same_row = owner_col[i] == owner_row[j]
                same_col = owner_col[j] == owner_row[i]
                if i == j:
                    same_row = same_row & (iota0 < iota1)
                    same_col = same_col & (iota1 < iota0)
                rank_row += jnp.sum(jnp.where(same_row, 1.0, 0.0), axis=0, keepdims=True)
                rank_col += jnp.sum(jnp.where(same_col, 1.0, 0.0), axis=1, keepdims=True)
            real = jnp.where(owner_col[j] >= 0, rank_col, 0.0)
            crowd = jnp.maximum(crowd, jnp.max(real, axis=0, keepdims=True))
            slot_row.append(owner_row[j] * width + rank_row.astype(jnp.int32))
            slot_col.append(owner_col[j] * width + rank_col.astype(jnp.int32))
    link_cond_col = [table2_t[:, 16 + j : 17 + j] for j in range(link_chunks)]
    set_send[...] = jnp.zeros(set_send.shape, F32)
    for i in range(n_dom * per_owner):
        held = jnp.full((1, LANES), -1.0, F32)
        total = jnp.zeros((1, LANES), F32)
        for j in range(link_chunks):
            here = (iota1 + LANES * i) == slot_col[j]
            local = (link_col[j] % shard).astype(F32)
            held = jnp.maximum(held, jnp.max(jnp.where(here, local, -1.0), axis=0, keepdims=True))
            total += jnp.sum(jnp.where(here, link_cond_col[j], 0.0), axis=0, keepdims=True)
            unpack[LANES * j : LANES * (j + 1), LANES * i : LANES * (i + 1)] = ones_where(here)
            pack[LANES * i : LANES * (i + 1), LANES * j : LANES * (j + 1)] = ones_where(
                (iota0 + LANES * i) == slot_row[j]
            )
        o, h = i // per_owner, i % per_owner
        set_send[o, h : h + 1, :] = held
        set_send[o, 2 + h : 3 + h, :] = total
    for o in range(n_dom):
        set_send[o, 4:5, :] = jnp.broadcast_to(crowd, (1, LANES))
    gain_send[...] = jnp.zeros(gain_send.shape, F32)
    for m in range(n_tm):
        chunk = pairs * (m % 2) + m // 2
        gain_send[m, 0:1, :] = gain_in_ref[chunk : chunk + 1, :]
        row = shard_chunks * me_d + m * shard_chunks // n_tm
        gain_send[m, 1:2, :] = gain_sh_ref[pl.ds(row, 1), :]

    pl.semaphore_wait(barrier, n_dom - 1 + n_tm - 1)
    for step in range(1, n_dom):
        dom_copy(SETUP, step, set_send.at[dom_peer(step)], set_recv.at[me_d]).start()
    for step in range(1, n_tm):
        tm_copy(0, step, gain_send.at[tm_peer(step)], gain_recv.at[me_t]).start()
    pair_copy(0, gain_in_ref.at[pl.ds(pairs * (1 - core), pairs)], pair_gain).start()
    set_recv[me_d] = set_send[me_d]
    gain_recv[me_t] = gain_send[me_t]

    lanes_of = lax.broadcasted_iota(jnp.int32, (LANES, bucket_nodes), 1)
    for j in range(link_chunks):
        across = slice(LANES * j, LANES * (j + 1))
        node_col = table2_t[:, j : j + 1].astype(jnp.int32)
        local = jnp.where(node_col >= 0, node_col % bucket_nodes, -1)
        node_cols[across, :] = ones_where(lanes_of == local)
        link_cond[across, :] = jnp.broadcast_to(link_cond_col[j], (LANES, LANES))
        mass_sum = jnp.zeros((LANES, LANES), F32)
        for i in range(w0_ref.shape[0] // LANES):
            here = iota1 + LANES * i == link_col[j]
            mass_sum += jnp.where(here, shared_mass_ref[i : i + 1, :], 0.0)
            shared_cols[across, LANES * i : LANES * (i + 1)] = ones_where(here)
        link_mass[across, :] = jnp.broadcast_to(jnp.sum(mass_sum, axis=1, keepdims=True), (LANES, LANES))
    span = bucket_rows.shape[2]
    block_iota = lax.broadcasted_iota(jnp.int32, (bsize, span), 0).astype(F32)
    eye = lax.broadcasted_iota(jnp.int32, (bsize, bsize), 0) == lax.broadcasted_iota(jnp.int32, (bsize, bsize), 1)
    scatter_parts[...] = jnp.zeros(scatter_parts.shape, BF16)
    per_bucket = bucket_nodes // bsize

    def cut(b, carry):
        held = bucket_rows[b // per_bucket]
        here = (block_iota + (b * bsize).astype(F32)) == held[0:1, :]
        own_cond = jnp.sum(jnp.where(here, held[1:2, :], 0.0), axis=1, keepdims=True)
        both = jnp.concatenate([jac_ref[b] + jnp.where(eye, own_cond, 0.0), off_ref[b]], axis=1)
        parts = split(both)
        blocks[b, :bsize, : 2 * bsize] = parts[:, :LANES]
        blocks[b, bsize:, : 2 * bsize] = parts[:, LANES:]
        blocks[b, :bsize, 2 * bsize :] = ones_where(here)
        blocks[b, bsize:, 2 * bsize :] = jnp.zeros((bsize, span), BF16)
        return carry

    lax.fori_loop(0, nblocks, cut, 0, unroll=2)

    each = LANES // bsize

    def begin(i, carry):
        at = rows(i * LANES, LANES)
        value = x0_ref[at, :]
        x[at, :] = value
        g_parts[pl.ds(i * each, each)] = split(value).reshape(each, bsize, 2 * LANES)
        return carry

    lax.fori_loop(0, chunks, begin, 0)
    x[at_sh : at_sh + shard, :] = w0_ref[rows(me_d * shard, shard), :]

    x[at_link:, :] = halves(dot(shared_cols[...], split(w0_ref[...])))

    for step in range(1, n_dom):
        dom_copy(SETUP, step, set_send.at[dom_peer(step)], set_recv.at[dom_source(step)]).wait_recv()
    for o in range(n_dom):
        for h in range(per_owner):
            at = o * per_owner + h
            table[at : at + 1, :] = set_recv[o, h : h + 1, :]
    table2_t[...] = table[...].T
    sums = [jnp.zeros((LANES, LANES), F32) for a in range(shard_chunks)]
    crowd = jnp.zeros((1, LANES), F32)
    for o in range(n_dom):
        crowd = jnp.maximum(crowd, set_recv[o, 4:5, :])
        for h in range(per_owner):
            i = o * per_owner + h
            held_row = set_recv[o, h : h + 1, :].astype(jnp.int32)
            held_col = table2_t[:, i : i + 1].astype(jnp.int32)
            for a in range(shard_chunks):
                here = (iota0 + LANES * a) == held_row
                sums[a] += jnp.where(here, set_recv[o, 2 + h : 3 + h, :], 0.0)
                own[LANES * a : LANES * (a + 1), LANES * i : LANES * (i + 1)] = ones_where(here)
                own_t[LANES * i : LANES * (i + 1), LANES * a : LANES * (a + 1)] = ones_where(
                    (iota1 + LANES * a) == held_col
                )
    for a in range(shard_chunks):
        total = column(COL_SHARED + 2 + a) + jnp.sum(sums[a], axis=1, keepdims=True)
        diag_sh[LANES * a : LANES * (a + 1), :] = jnp.broadcast_to(total, (LANES, LANES))
    flag_ref[...] = jnp.broadcast_to(crowd, flag_ref.shape)

    def apply(vec, parts, out, shifted=None):
        for t in range(nbuckets):
            at = slice(t * bucket_cap, (t + 1) * bucket_cap)
            flows = link_cond[at, :] * vec[at_link + at.start : at_link + at.stop, :]
            scatter_parts[t, :bucket_cap, :] = split(-flows)

        def one(b, carry):
            other = block_link_ref[b]
            at = rows(b * bsize, bsize)
            acc = dot(blocks[b], jnp.concatenate([parts[b], parts[other], scatter_parts[b // per_bucket]], axis=0))
            value = halves(acc[:bsize, :]) + acc[bsize:, :LANES]
            if shifted is not None:
                value = value - SHIFT * vec[at, :]
                shifted[b] = split(value)
            out[at, :] = value
            return carry

        lax.fori_loop(0, nblocks, one, 0, unroll=4)

    def gather_flow(parts):
        blocks_in = bucket_nodes // bsize
        for t in range(nbuckets):
            at = slice(t * bucket_cap, (t + 1) * bucket_cap)
            chunk = parts[t * blocks_in : (t + 1) * blocks_in].reshape(bucket_nodes, 2 * LANES)
            value = halves(dot(node_cols[at, :], chunk)) * link_cond[at, :]
            flow_parts[at, :] = split(value)

    def start_exchange(kind):
        for step in range(1, n_dom):
            dom_copy(
                kind,
                step,
                stage.at[kind, dom_peer(step), pl.ds(0, cap)],
                recv.at[kind, me_d, pl.ds(0, cap)],
            ).start()
        recv[kind, me_d] = stage[kind, me_d]

    def wait_exchange(kind, receive):
        for step in range(1, n_dom):
            copy = dom_copy(
                kind,
                step,
                stage.at[kind, dom_peer(step), pl.ds(0, cap)],
                recv.at[kind, dom_source(step), pl.ds(0, cap)],
            )
            if receive:
                copy.wait_recv()
            else:
                copy.wait_send()

    def fill_stage(kind, matrix, value_parts):
        some = n_dom // 2

        def one(i, carry):
            got = halves(dot(matrix[rows(i * some * width, some * width), :], value_parts))
            stage[kind, pl.ds(i * some, some)] = got.reshape(some, width, LANES)
            return carry

        lax.fori_loop(0, 2, one, 0)
        start_exchange(kind)

    def send_flow(kind, parts):
        gather_flow(parts)
        fill_stage(kind, pack, flow_parts[...])

    def load_slots(kind):
        for o in range(n_dom):
            slot_parts[o * width : (o + 1) * width, :] = split(recv[kind, o])

    def collect_flow(kind):
        wait_exchange(kind, True)
        load_slots(kind)
        return halves(dot(own[...], slot_parts[...]))

    def send_back(kind, value):
        fill_stage(kind, own_t, split(value))

    def take_back(kind, out):
        wait_exchange(kind, True)
        load_slots(kind)
        out[at_link : at_link + links, :] = halves(dot(unpack[...], slot_parts[...]))

    def set_fixed(k):
        for i in range(chunks):
            at = slice(LANES * i, LANES * (i + 1))
            drive = amp_ref[at, :] * column(COL_SIN + chunks * k + i)
            fixed[at, :] = column(COL_MASS + i) * x[at, :] + drive
        for a in range(shard_chunks):
            at = slice(at_sh + LANES * a, at_sh + LANES * (a + 1))
            fixed[at, :] = column(COL_SHARED + a) * x[at, :]
        fixed[at_link:, :] = link_mass[...] * x[at_link:, :]

    def residual_nodes():
        def one(i, carry):
            at = rows(i * LANES, LANES)
            value = fixed[at, :] - jx[at, :] - nonlin_ref[...] * jnp.tanh(x[at, :])
            g[at, :] = value
            g_parts[pl.ds(i * each, each)] = split(value).reshape(each, bsize, 2 * LANES)
            return carry

        lax.fori_loop(0, chunks, one, 0)

    at = slice(at_sh, at_sh + shard)

    def residual_shared(where):
        g[where, :] = fixed[where, :] - jx[where, :]

    def shifted_shared():
        p[at, :] = (diag_sh[...] - SHIFT) * g[at, :] - collect_flow(FLOW_G)
        send_back(BACK_P, p[at, :])

    def start_shared():
        jx[at, :] = diag_sh[...] * x[at, :] - collect_flow(FLOW_P)
        send_back(BACK_Q, jx[at, :])
        residual_shared(at)
        shifted_shared()
        take_back(BACK_Q, jx)
        residual_shared(slice(at_link, at_link + links))
        for kind in (FLOW_P, BACK_Q):
            wait_exchange(kind, False)

    def newton(turn, carry):
        send_flow(FLOW_G, g_parts)
        pl.when(turn == 0)(start_shared)
        apply(g, g_parts, p, p_parts)
        send_flow(FLOW_P, p_parts)
        pl.when(turn > 0)(shifted_shared)

        def sum_over(i, sums, pairs):
            return tuple(
                s + jnp.sum((a * b).reshape(LANES // 8, 8, LANES), axis=0)
                for s, (a, b) in zip(sums, pairs)
            )

        def gram_early(i, sums):
            here = rows(i * LANES, LANES)
            vg, vp = g[here, :], p[here, :]
            return sum_over(i, sums, ((vg, vg), (vg, vp), (vp, vp)))

        def gram_late(i, sums):
            here = rows(i * LANES, LANES)
            vg, vp, vq = g[here, :], p[here, :], q[here, :]
            return sum_over(i, sums, ((vg, vq), (vp, vq), (vq, vq)))

        zero = (jnp.zeros((8, LANES), F32),) * 3
        early = lax.fori_loop(0, chunks + shard_chunks, gram_early, zero)
        q[at, :] = diag_sh[...] * p[at, :] - collect_flow(FLOW_P)
        send_back(BACK_Q, q[at, :])
        take_back(BACK_P, p)
        apply(p, p_parts, q)
        late = lax.fori_loop(0, chunks + shard_chunks, gram_late, zero)
        sums = early + late
        for i, s in enumerate(sums):
            gram_send[i : i + 1, :] = jnp.sum(s, axis=0, keepdims=True)
        gram_send[6:8, :] = jnp.zeros((2, LANES), F32)
        for step in range(1, n_dom):
            dom_copy(GRAM, step, gram_send, gram_recv.at[me_d]).start()
        gram_recv[me_d] = gram_send[...]
        for kind in (FLOW_G, FLOW_P, BACK_P, BACK_Q):
            wait_exchange(kind, False)
        for step in range(1, n_dom):
            copy = dom_copy(GRAM, step, gram_send, gram_recv.at[dom_source(step)])
            copy.wait_send()
            copy.wait_recv()
        total = gram_recv[0]
        for o in range(1, n_dom):
            total = total + gram_recv[o]
        gg, gp, pp, gq, pq, qq = [total[i : i + 1, :] for i in range(6)]
        norm2 = gg + 1e-30
        inv2 = 1.0 / norm2
        h00 = (gp + SHIFT * gg) * inv2
        turnover = h00 - SHIFT
        tail2 = pp - 2.0 * turnover * gp + turnover * turnover * gg
        inv_both = 1.0 / (jnp.sqrt(norm2) * jnp.sqrt(tail2))
        inv_tail2 = 1.0 / tail2
        push = turnover * SHIFT
        g_s = gq - turnover * gp - push * gg
        p_s = pq - turnover * pp - push * gp
        q_s = qq - turnover * pq - push * gq
        t_s = p_s - turnover * g_s
        s_s = q_s - turnover * p_s - push * g_s
        g_t = gp - turnover * gg
        h10 = tail2 * inv_both
        h01 = g_s * inv_both
        h11 = t_s * inv_tail2
        h21_2 = (
            s_s * inv_tail2
            - h01 * h01 * (2.0 - gg * inv2)
            - h11 * h11
            + 2.0 * h01 * h11 * g_t * inv_both
        )
        n11 = h00 * h00 + h10 * h10
        n12 = h00 * h01 + h10 * h11
        n22 = h01 * h01 + h11 * h11 + h21_2
        inv_det = 1.0 / (n11 * n22 - n12 * n12)
        c_p = norm2 * inv_both * (h01 * n11 - h00 * n12) * inv_det
        c_g = (h00 * n22 - h01 * n12) * inv_det - turnover * c_p

        def advance(here):
            vg, vp = g[here, :], p[here, :]
            x[here, :] = x[here, :] + c_g * vg + c_p * vp
            jx[here, :] = jx[here, :] + c_g * (vp + SHIFT * vg) + c_p * q[here, :]

        def one(i, carry):
            advance(rows(i * LANES, LANES))
            return carry

        lax.fori_loop(0, chunks + shard_chunks, one, 0)
        take_back(BACK_Q, q)
        advance(slice(at_link, at_link + links))

        @pl.when(turn == NEWTON - 1)
        def _():
            set_fixed(1)

        @pl.when(turn < FINE * NEWTON - 1)
        def _():
            residual_nodes()
            residual_shared(slice(at_sh, at_link + links))

        return carry

    send_flow(FLOW_P, g_parts)
    apply(x, g_parts, jx)
    set_fixed(0)
    residual_nodes()
    lax.fori_loop(0, FINE * NEWTON, newton, 0)

    per_rows, per_shared = nodes // n_tm, shard // n_tm
    for a in range(shard_chunks):
        here = slice(at_sh + LANES * a, at_sh + LANES * (a + 1))
        start = w0_ref[rows(me_d * shard + LANES * a, LANES), :]
        jump = x[here, :] - column(COL_SHARED + 4 + a) * start
        pieces = LANES // per_shared
        for m in range(pieces):
            jump_sh_send[a * pieces + m] = jump[per_shared * m : per_shared * (m + 1), :]
    for step in range(1, n_tm):
        tm_copy(3, step, jump_sh_send.at[tm_peer(step)], jump_sh_recv.at[me_t]).start()
    jump_sh_recv[me_t] = jump_sh_send[me_t]
    for i in range(chunks):
        here = slice(LANES * i, LANES * (i + 1))
        jump_send[i] = x[here, :] - column(COL_GAIN + i) * x0_ref[here, :]
    pair_copy(1, jump_send.at[pl.ds(pairs * (1 - core), pairs)], pair_jump).start()
    pair_copy(0, gain_in_ref.at[pl.ds(pairs * (1 - core), pairs)], pair_gain).wait_recv()
    for step in range(1, n_tm):
        tm_copy(0, step, gain_send.at[tm_peer(step)], gain_recv.at[tm_source(step)]).wait_recv()
    for m in range(n_tm):
        table[m : m + 1, :] = gain_recv[m, 0:1, :]
        table[n_tm + m : n_tm + m + 1, :] = gain_recv[m, 1:2, :]
    first_core = core == 0
    own_gain, other_gain = gain_in_ref[pl.ds(pairs * core, pairs), :], pair_gain[...]
    table[2 * n_tm : 2 * n_tm + pairs, :] = jnp.where(first_core, own_gain, other_gain)
    table[3 * n_tm : 3 * n_tm + pairs, :] = jnp.where(first_core, other_gain, own_gain)
    table2_t[...] = table[...].T
    my_shared = rows(lax.rem(me_t, LANES // per_shared) * per_shared, per_shared)

    def map_copy(step, holder):
        return chip_copy(1, step, value_send.at[chip_peer(step)], jump_recv.at[holder])

    def value_copy(step, holder):
        return chip_copy(2, step, jump_recv.at[pairs + chip_peer(step)], value_recv.at[holder])

    def shared_copy(step, holder):
        return tm_copy(
            7, step, value_sh_send.at[tm_peer(step)], value_sh.at[rows(holder * per_shared, per_shared)]
        )

    def solve(gains, jumps, values):
        whole, total = gains[0], jumps[0]
        for m in range(1, len(gains)):
            whole = whole * gains[m]
            total = gains[m] * total + jumps[m]
        value = total / (1.0 - whole)
        for m in range(len(gains)):
            values[m] = value
            if m + 1 < len(gains):
                value = gains[m] * value + jumps[m]

    def pair_slices(i):
        mine, other = jump_send[pairs * core + i], pair_jump[i]
        return jnp.where(first_core, mine, other), jnp.where(first_core, other, mine)

    pair_copy(1, jump_send.at[pl.ds(pairs * (1 - core), pairs)], pair_jump).wait_recv()
    for i in range(pairs):
        first, second = pair_slices(i)
        value_send[i] = table2_t[:, 3 * n_tm + i : 3 * n_tm + i + 1] * first + second
    for step in range(1, pairs):
        map_copy(step, chip).start()
    jump_recv[chip] = value_send[chip]
    for step in range(1, n_tm):
        tm_copy(3, step, jump_sh_send.at[tm_peer(step)], jump_sh_recv.at[tm_source(step)]).wait_recv()
    solve([table2_t[my_shared, n_tm + m : n_tm + m + 1] for m in range(n_tm)], jump_sh_recv, value_sh_send)
    for step in range(1, n_tm):
        shared_copy(step, me_t).start()
    value_sh[rows(me_t * per_shared, per_shared), :] = value_sh_send[me_t]
    for step in range(1, pairs):
        map_copy(step, chip_source(step)).wait_recv()
    pair_gains = [table2_t[:, 2 * k : 2 * k + 1] * table2_t[:, 2 * k + 1 : 2 * k + 2] for k in range(pairs)]
    solve(pair_gains, jump_recv, jump_recv.at[pl.ds(pairs, pairs)])
    for step in range(1, pairs):
        value_copy(step, chip).start()
    value_recv[chip] = jump_recv[pairs + chip]
    for step in range(1, n_tm):
        shared_copy(step, tm_source(step)).wait_recv()
    for step in range(1, n_dom):
        dom_copy(LAST, step, value_sh, out_sh_ref.at[rows(me_d * shard, shard)]).start()
    out_sh_ref[rows(me_d * shard, shard), :] = value_sh[...]
    for step in range(1, pairs):
        value_copy(step, chip_source(step)).wait_recv()
    half = nodes // 2
    for i in range(pairs):
        first, second = pair_slices(i)
        even = value_recv[i]
        odd = table2_t[:, 2 * n_tm + i : 2 * n_tm + i + 1] * even + first
        out_in_ref[rows(half * core + LANES * i, LANES), :] = jnp.where(first_core, even, odd)
        pair_value[LANES * i : LANES * (i + 1), :] = jnp.where(first_core, odd, even)
    pair_copy(2, pair_value, out_in_ref.at[rows(half * core, half)]).start()
    pair_copy(2, pair_value, out_in_ref.at[rows(half * (1 - core), half)]).wait_recv()
    for step in range(1, n_dom):
        copy = dom_copy(LAST, step, value_sh, out_sh_ref.at[rows(dom_source(step) * shard, shard)])
        copy.wait_recv()
        copy.wait_send()
        dom_copy(SETUP, step, set_send.at[dom_peer(step)], set_recv.at[me_d]).wait_send()
    for step in range(1, n_tm):
        tm_copy(0, step, gain_send.at[tm_peer(step)], gain_recv.at[me_t]).wait_send()
        tm_copy(3, step, jump_sh_send.at[tm_peer(step)], jump_sh_recv.at[me_t]).wait_send()
        shared_copy(step, me_t).wait_send()
    for step in range(1, pairs):
        map_copy(step, chip).wait_send()
        value_copy(step, chip).wait_send()
    pair_copy(0, gain_in_ref.at[pl.ds(pairs * (1 - core), pairs)], pair_gain).wait_send()
    pair_copy(1, jump_send.at[pl.ds(pairs * (1 - core), pairs)], pair_jump).wait_send()
    pair_copy(2, pair_value, out_in_ref.at[rows(half * core, half)]).wait_send()


def run(cap, width, bucket_nodes, bucket_cap, collective_id, n_tm, n_dom, operands):
    nodes, samples = operands[0].shape
    shared = operands[1].shape[0]
    shard = shared // n_dom
    nbuckets = nodes // bucket_nodes
    links = nbuckets * bucket_cap
    span = -(-bucket_cap // LANES) * LANES
    nblocks, bsize = operands[4].shape[0], operands[4].shape[1]
    total = nodes + shard + links
    slots = n_dom * width
    vmem = pl.BlockSpec(memory_space=pltpu.VMEM)
    smem = pl.BlockSpec(memory_space=pltpu.SMEM)
    specs = [vmem] * len(operands)
    specs[6] = smem
    state = pltpu.VMEM((total, samples), F32)
    tile = pltpu.VMEM((LANES, LANES), F32)
    return pl.pallas_call(
        functools.partial(kernel, cap, width, bucket_nodes, bucket_cap, n_tm, n_dom),
        out_shape=(
            jax.ShapeDtypeStruct((nodes, samples), F32),
            jax.ShapeDtypeStruct((shared, samples), F32),
            jax.ShapeDtypeStruct((8, LANES), F32),
        ),
        in_specs=specs,
        out_specs=(vmem, vmem, vmem),
        scratch_shapes=[
            state,
            state,
            state,
            state,
            state,
            state,
            pltpu.VMEM((nblocks, bsize, 2 * samples), BF16),
            pltpu.VMEM((nblocks, bsize, 2 * samples), BF16),
            pltpu.VMEM((links, 2 * samples), BF16),
            pltpu.VMEM((slots, 2 * samples), BF16),
            pltpu.VMEM((nblocks, 2 * bsize, 2 * bsize + span), BF16),
            pltpu.VMEM((links, bucket_nodes), BF16),
            pltpu.VMEM((nbuckets, 8, span), F32),
            pltpu.VMEM((nbuckets, span, 2 * samples), BF16),
            pltpu.VMEM((links, shared), BF16),
            pltpu.VMEM((slots, links), BF16),
            pltpu.VMEM((links, slots), BF16),
            pltpu.VMEM((shard, slots), BF16),
            pltpu.VMEM((slots, shard), BF16),
            tile,
            tile,
            tile,
            pltpu.VMEM((links, samples), F32),
            pltpu.VMEM((links, samples), F32),
            pltpu.VMEM((shard, samples), F32),
            pltpu.VMEM((4, n_dom, width, samples), F32),
            pltpu.VMEM((4, n_dom, width, samples), F32),
            pltpu.VMEM((n_dom, 8, LANES), F32),
            pltpu.VMEM((n_dom, 8, LANES), F32),
            pltpu.VMEM((n_tm, 8, LANES), F32),
            pltpu.VMEM((n_tm, 8, LANES), F32),
            pltpu.VMEM((8, LANES), F32),
            pltpu.VMEM((n_dom, 8, LANES), F32),
            pltpu.VMEM((n_tm, nodes // n_tm, samples), F32),
            pltpu.VMEM((n_tm, nodes // n_tm, samples), F32),
            pltpu.VMEM((n_tm, nodes // n_tm, samples), F32),
            pltpu.VMEM((n_tm, shard // n_tm, samples), F32),
            pltpu.VMEM((n_tm, shard // n_tm, samples), F32),
            pltpu.VMEM((n_tm, shard // n_tm, samples), F32),
            pltpu.VMEM((n_tm // 2, LANES), F32),
            pltpu.VMEM((n_tm // 2, LANES, samples), F32),
            pltpu.VMEM((nodes // 2, samples), F32),
            pltpu.VMEM((n_tm // 2, LANES, samples), F32),
            pltpu.VMEM((shard, samples), F32),
            pltpu.SemaphoreType.DMA((7, n_dom)),
            pltpu.SemaphoreType.DMA((7, n_dom)),
            pltpu.SemaphoreType.DMA((8, n_tm)),
            pltpu.SemaphoreType.DMA((8, n_tm)),
        ],
        compiler_params=pltpu.CompilerParams(
            collective_id=collective_id, has_side_effects=True, vmem_limit_bytes=62 * 1024 * 1024
        ),
        name="parareal",
    )(*operands)


def shards(
    state_interior,
    state_shared,
    gain_interior,
    gain_shared,
    jac_blocks,
    off_blocks,
    block_link,
    mass,
    shared_mass,
    shared_diag,
    link_node,
    link_shared,
    link_cond,
    source_amp,
    phase,
    nonlin,
):
    n_tm, n_dom = lax.axis_size("tm"), lax.axis_size("dom")

    def lanes(value):
        return value.reshape(-1, LANES)

    operands = (
        state_interior[0],
        state_shared[0],
        lanes(gain_interior),
        lanes(gain_shared),
        jac_blocks,
        off_blocks,
        block_link,
        lanes(mass),
        lanes(shared_mass),
        lanes(shared_diag),
        lanes(link_node),
        lanes(link_shared),
        lanes(link_cond),
        source_amp,
        lanes(phase),
        lanes(nonlin),
    )
    nodes, shard = state_interior.shape[1], state_shared.shape[1] // n_dom
    new_in, new_sh, crowd = run(SLOTS, LANES, 2 * LANES, SLOTS, 0, n_tm, n_dom, operands)
    new_in, new_sh = lax.cond(
        jnp.max(crowd) < SLOTS,
        lambda: (new_in, new_sh),
        lambda: run(shard, shard, nodes, link_node.shape[0], 1, n_tm, n_dom, operands)[:2],
    )
    return (new_in[None], new_sh[None])


def solution(mesh):
    return jax.shard_map(
        shards,
        mesh=mesh,
        in_specs=(
            P("tm", "dom", None),
            P("tm", None, None),
            P("tm", "dom"),
            P("tm", None),
            P("dom", None, None),
            P("dom", None, None),
            P("dom"),
            P("dom"),
            P(),
            P(),
            P("dom"),
            P("dom"),
            P("dom"),
            P("dom", None),
            P("dom"),
            P(),
        ),
        out_specs=(P("tm", "dom", None), P("tm", None, None)),
        check_vma=False,
    )
```

```python
import functools
import math

import jax
import jax.numpy as jnp
from jax import lax
from jax.experimental import pallas as pl
from jax.experimental.pallas import tpu as pltpu
from jax.sharding import PartitionSpec as P

FINE = 2
NEWTON = 2
SHIFT = 8.0
SLOTS = 96
LANES = 128
MESH = pl.DeviceIdType.MESH
F32 = jnp.float32
BF16 = jnp.bfloat16

COL_MASS, COL_SIN, COL_GAIN, COL_SHARED, COL_NODE, COL_LINK, COL_COND = 0, 16, 48, 64, 72, 80, 88
ABSENT = 2.0**20
FLOW_G, FLOW_P, BACK_P, BACK_Q, SETUP, GRAM, LAST = range(7)


def halves(acc):
    return acc[:, :LANES] + acc[:, LANES:]


def split(value):
    high = value.astype(BF16)
    low = (value - high.astype(F32)).astype(BF16)
    return jnp.concatenate([high, low], axis=1)


def dot(a, b):
    return jnp.dot(a, b, preferred_element_type=F32)


def ones_where(mask):
    return jnp.where(mask, 1.0, 0.0).astype(BF16)


def kernel(
    cap,
    width,
    bucket_nodes,
    bucket_cap,
    n_tm,
    n_dom,
    x0_hbm,
    w0_hbm,
    gain_in_ref,
    gain_sh_ref,
    jac_hbm,
    off_hbm,
    block_link_ref,
    mass_ref,
    shared_mass_ref,
    shared_diag_ref,
    node_ref,
    link_ref,
    cond_ref,
    amp_hbm,
    phase_ref,
    nonlin_ref,
    out_in_ref,
    out_sh_ref,
    flag_ref,
    x0_ref,
    w0_ref,
    jac_ref,
    off_ref,
    amp_ref,
    load_sem,
    x,
    jx,
    g,
    p,
    q,
    fixed,
    g_parts,
    p_parts,
    flow_parts,
    slot_parts,
    blocks,
    node_cols,
    node_rows,
    bucket_rows,
    scatter_parts,
    shared_cols,
    pack,
    unpack,
    own,
    own_t,
    table,
    table_t,
    table2_t,
    link_mass,
    link_cond,
    diag_sh,
    stage,
    recv,
    set_send,
    set_recv,
    gain_send,
    gain_recv,
    gram_send,
    gram_recv,
    jump_send,
    jump_recv,
    value_send,
    jump_sh_send,
    jump_sh_recv,
    value_sh_send,
    pair_gain,
    pair_jump,
    pair_value,
    value_recv,
    value_sh,
    send_sem,
    recv_sem,
    tm_send,
    tm_recv,
):
    me_t, me_d = lax.axis_index("tm"), lax.axis_index("dom")
    nodes = x0_ref.shape[0]
    shard = w0_ref.shape[0] // n_dom
    links = flow_parts.shape[0]
    chunks, shard_chunks, link_chunks = nodes // LANES, shard // LANES, links // LANES
    at_sh, at_link = nodes, nodes + shard
    per_owner = width // LANES
    nblocks, bsize = jac_ref.shape[0], jac_ref.shape[1]
    iota0 = lax.broadcasted_iota(jnp.int32, (LANES, LANES), 0)
    iota1 = lax.broadcasted_iota(jnp.int32, (LANES, LANES), 1)

    def rows(start, size):
        return pl.ds(pl.multiple_of(start, size), size)

    def dom_peer(step):
        return lax.rem(me_d + step, n_dom)

    def dom_source(step):
        return lax.rem(me_d + n_dom - step, n_dom)

    def tm_peer(step):
        return lax.rem(me_t + step, n_tm)

    def tm_source(step):
        return lax.rem(me_t + n_tm - step, n_tm)

    def dom_copy(kind, step, source, target):
        return pltpu.make_async_remote_copy(
            src_ref=source,
            dst_ref=target,
            send_sem=send_sem.at[kind, step],
            recv_sem=recv_sem.at[kind, step],
            device_id={"dom": dom_peer(step)},
            device_id_type=MESH,
        )

    def tm_copy(kind, step, source, target):
        return pltpu.make_async_remote_copy(
            src_ref=source,
            dst_ref=target,
            send_sem=tm_send.at[kind, step],
            recv_sem=tm_recv.at[kind, step],
            device_id={"tm": tm_peer(step)},
            device_id_type=MESH,
        )

    pairs = n_tm // 2
    core, chip = lax.rem(me_t, 2), me_t // 2

    def pair_copy(kind, source, target):
        return pltpu.make_async_remote_copy(
            src_ref=source,
            dst_ref=target,
            send_sem=tm_send.at[4 + kind, 0],
            recv_sem=tm_recv.at[4 + kind, 0],
            device_id={"tm": me_t + 1 - 2 * core},
            device_id_type=MESH,
        )

    def chip_peer(step):
        return lax.rem(chip + step, pairs)

    def chip_source(step):
        return lax.rem(chip + pairs - step, pairs)

    def chip_copy(kind, step, source, target):
        return pltpu.make_async_remote_copy(
            src_ref=source,
            dst_ref=target,
            send_sem=tm_send.at[kind, step],
            recv_sem=tm_recv.at[kind, step],
            device_id={"tm": 2 * chip_peer(step) + core},
            device_id_type=MESH,
        )

    far_first = sorted(range(1, n_dom), key=lambda step: (step % 2 == 0, abs(2 * step - n_dom)))
    far_chips = sorted(range(1, pairs), key=lambda step: (step % 2 == 0, abs(2 * step - pairs)))

    loads = [
        pltpu.make_async_copy(source, target, load_sem.at[i])
        for i, (source, target) in enumerate(
            (
                (jac_hbm, jac_ref),
                (off_hbm, off_ref),
                (x0_hbm, x0_ref),
                (w0_hbm, w0_ref),
                (amp_hbm, amp_ref),
            )
        )
    ]
    for load in loads:
        load.start()

    if cap < width:
        for kind in range(4):
            for o in range(n_dom):
                recv[kind, o, cap:, :] = jnp.zeros((width - cap, LANES), F32)
    barrier = pltpu.get_barrier_semaphore()
    for step in range(1, n_dom):
        pl.semaphore_signal(barrier, inc=1, device_id={"dom": dom_peer(step)}, device_id_type=MESH)
    for step in range(1, n_tm):
        pl.semaphore_signal(barrier, inc=1, device_id={"tm": tm_peer(step)}, device_id_type=MESH)

    slice_f = me_t.astype(F32)
    table[...] = jnp.zeros((LANES, LANES), F32)
    table[COL_MASS : COL_MASS + chunks, :] = mass_ref[...]
    for k in range(FINE):
        angle = (slice_f * FINE + (k + 1.0)) * (2.0 * math.pi / (n_tm * FINE))
        at = COL_SIN + chunks * k
        table[at : at + chunks, :] = jnp.sin(angle + phase_ref[...])
    table[COL_GAIN : COL_GAIN + chunks, :] = gain_in_ref[...]
    for a in range(shard_chunks):
        row = shard_chunks * me_d + a
        table[COL_SHARED + a : COL_SHARED + a + 1, :] = shared_mass_ref[pl.ds(row, 1), :]
        table[COL_SHARED + 2 + a : COL_SHARED + 3 + a, :] = shared_diag_ref[pl.ds(row, 1), :]
        table[COL_SHARED + 4 + a : COL_SHARED + 5 + a, :] = gain_sh_ref[pl.ds(row, 1), :]
    given = node_ref.shape[0]
    table[COL_NODE : COL_NODE + given, :] = node_ref[...].astype(F32)
    table[COL_LINK : COL_LINK + given, :] = link_ref[...].astype(F32)
    table[COL_COND : COL_COND + given, :] = cond_ref[...]
    table_t[...] = table[...].T

    def column(at):
        return table_t[:, at : at + 1]

    nbuckets = nodes // bucket_nodes
    bucket_rows[...] = jnp.zeros(bucket_rows.shape, F32)
    crowd = jnp.zeros((1, 1), F32)
    if nbuckets == 1:
        for j in range(given):
            across = slice(LANES * j, LANES * (j + 1))
            bucket_rows[0, 0:1, across] = node_ref[j : j + 1, :].astype(F32)
            bucket_rows[0, 1:2, across] = cond_ref[j : j + 1, :]
        table[0:given, :] = node_ref[...].astype(F32)
        table[8 : 8 + given, :] = link_ref[...].astype(F32)
        table[16 : 16 + given, :] = cond_ref[...]
    else:
        given_node = [column(COL_NODE + j) for j in range(given)]
        given_link = [column(COL_LINK + j) for j in range(given)]
        given_cond = [column(COL_COND + j) for j in range(given)]
        bucket_col = [v.astype(jnp.int32) // bucket_nodes for v in given_node]
        bucket_row = [node_ref[j : j + 1, :] // bucket_nodes for j in range(given)]
        place = []
        for j in range(given):
            rank = jnp.zeros((LANES, 1), F32)
            for i in range(j + 1):
                same = bucket_col[j] == bucket_row[i]
                if i == j:
                    same = same & (iota1 < iota0)
                rank += jnp.sum(jnp.where(same, 1.0, 0.0), axis=1, keepdims=True)
            crowd = jnp.maximum(crowd, jnp.max(rank, axis=0, keepdims=True))
            place.append((bucket_col[j], rank.astype(jnp.int32)))

        def picked(masks, values, none):
            total = jnp.zeros((1, LANES), F32)
            for mask, value in zip(masks, values):
                total += jnp.sum(jnp.where(mask, value + none, 0.0), axis=0, keepdims=True)
            return total - none

        for i in range(nbuckets):
            masks = [(b == i) & (iota1 == r) for b, r in place]
            bucket_rows[i, 0:1, :] = picked(masks, given_node, ABSENT)
            bucket_rows[i, 1:2, :] = picked(masks, given_cond, 0.0)
        for i in range(link_chunks):
            masks = [(iota1 + LANES * i) == b * bucket_cap + r for b, r in place]
            table[i : i + 1, :] = picked(masks, given_node, ABSENT)
            table[8 + i : 9 + i, :] = picked(masks, given_link, ABSENT)
            table[16 + i : 17 + i, :] = picked(masks, given_cond, 0.0)
    table2_t[...] = table[...].T

    link_col = [table2_t[:, 8 + j : 9 + j].astype(jnp.int32) for j in range(link_chunks)]
    link_row = [table[8 + j : 9 + j, :].astype(jnp.int32) for j in range(link_chunks)]
    if cap == width:
        slot_col, slot_row = link_col, link_row
    else:
        owner_col = [v // shard for v in link_col]
        owner_row = [v // shard for v in link_row]
        slot_col, slot_row = [], []
        for j in range(link_chunks):
            rank_row = jnp.zeros((1, LANES), F32)
            rank_col = jnp.zeros((LANES, 1), F32)
            for i in range(j + 1):
                same_row = owner_col[i] == owner_row[j]
                same_col = owner_col[j] == owner_row[i]
                if i == j:
                    same_row = same_row & (iota0 < iota1)
                    same_col = same_col & (iota1 < iota0)
                rank_row += jnp.sum(jnp.where(same_row, 1.0, 0.0), axis=0, keepdims=True)
                rank_col += jnp.sum(jnp.where(same_col, 1.0, 0.0), axis=1, keepdims=True)
            real = jnp.where(owner_col[j] >= 0, rank_col, 0.0)
            crowd = jnp.maximum(crowd, jnp.max(real, axis=0, keepdims=True))
            slot_row.append(owner_row[j] * width + rank_row.astype(jnp.int32))
            slot_col.append(owner_col[j] * width + rank_col.astype(jnp.int32))
    link_cond_col = [table2_t[:, 16 + j : 17 + j] for j in range(link_chunks)]
    set_send[...] = jnp.zeros(set_send.shape, F32)
    for i in range(n_dom * per_owner):
        held = jnp.full((1, LANES), -1.0, F32)
        total = jnp.zeros((1, LANES), F32)
        for j in range(link_chunks):
            here = (iota1 + LANES * i) == slot_col[j]
            local = (link_col[j] % shard).astype(F32)
            held = jnp.maximum(held, jnp.max(jnp.where(here, local, -1.0), axis=0, keepdims=True))
            total += jnp.sum(jnp.where(here, link_cond_col[j], 0.0), axis=0, keepdims=True)
            unpack[LANES * j : LANES * (j + 1), LANES * i : LANES * (i + 1)] = ones_where(here)
            pack[LANES * i : LANES * (i + 1), LANES * j : LANES * (j + 1)] = ones_where(
                (iota0 + LANES * i) == slot_row[j]
            )
        o, h = i // per_owner, i % per_owner
        set_send[o, h : h + 1, :] = held
        set_send[o, 2 + h : 3 + h, :] = total
    for o in range(n_dom):
        set_send[o, 4:5, :] = jnp.broadcast_to(crowd, (1, LANES))
    gain_send[...] = jnp.zeros(gain_send.shape, F32)
    for m in range(n_tm):
        chunk = pairs * (m % 2) + m // 2
        gain_send[m, 0:1, :] = gain_in_ref[chunk : chunk + 1, :]
        row = shard_chunks * me_d + m * shard_chunks // n_tm
        gain_send[m, 1:2, :] = gain_sh_ref[pl.ds(row, 1), :]

    pl.semaphore_wait(barrier, n_dom - 1 + n_tm - 1)
    for step in range(1, n_dom):
        dom_copy(SETUP, step, set_send.at[dom_peer(step)], set_recv.at[me_d]).start()
    for step in range(1, n_tm):
        tm_copy(0, step, gain_send.at[tm_peer(step)], gain_recv.at[me_t]).start()
    pair_copy(0, gain_in_ref.at[pl.ds(pairs * (1 - core), pairs)], pair_gain).start()
    set_recv[me_d] = set_send[me_d]
    gain_recv[me_t] = gain_send[me_t]

    lanes_of = lax.broadcasted_iota(jnp.int32, (LANES, bucket_nodes), 1)
    for j in range(link_chunks):
        across = slice(LANES * j, LANES * (j + 1))
        node_col = table2_t[:, j : j + 1].astype(jnp.int32)
        local = jnp.where(node_col >= 0, node_col % bucket_nodes, -1)
        node_cols[across, :] = ones_where(lanes_of == local)
        link_cond[across, :] = jnp.broadcast_to(link_cond_col[j], (LANES, LANES))
        mass_sum = jnp.zeros((LANES, LANES), F32)
        for i in range(w0_ref.shape[0] // LANES):
            here = iota1 + LANES * i == link_col[j]
            mass_sum += jnp.where(here, shared_mass_ref[i : i + 1, :], 0.0)
            shared_cols[across, LANES * i : LANES * (i + 1)] = ones_where(here)
        link_mass[across, :] = jnp.broadcast_to(jnp.sum(mass_sum, axis=1, keepdims=True), (LANES, LANES))
    span = bucket_rows.shape[2]
    block_iota = lax.broadcasted_iota(jnp.int32, (bsize, span), 0).astype(F32)
    eye = lax.broadcasted_iota(jnp.int32, (bsize, bsize), 0) == lax.broadcasted_iota(jnp.int32, (bsize, bsize), 1)
    scatter_parts[...] = jnp.zeros(scatter_parts.shape, BF16)
    per_bucket = bucket_nodes // bsize

    for load in loads:
        load.wait()

    def cut(b, carry):
        held = bucket_rows[b // per_bucket]
        here = (block_iota + (b * bsize).astype(F32)) == held[0:1, :]
        own_cond = jnp.sum(jnp.where(here, held[1:2, :], 0.0), axis=1, keepdims=True)
        both = jnp.concatenate([jac_ref[b] + jnp.where(eye, own_cond, 0.0), off_ref[b]], axis=1)
        parts = split(both)
        blocks[b, :bsize, : 2 * bsize] = parts[:, :LANES]
        blocks[b, bsize:, : 2 * bsize] = parts[:, LANES:]
        places = ones_where(here)
        blocks[b, :bsize, 2 * bsize :] = places
        node_rows[rows(b * bsize, bsize), :] = places
        blocks[b, bsize:, 2 * bsize :] = jnp.zeros((bsize, span), BF16)
        return carry

    lax.fori_loop(0, nblocks, cut, 0, unroll=2)

    each = LANES // bsize

    def begin(i, carry):
        at = rows(i * LANES, LANES)
        value = x0_ref[at, :]
        x[at, :] = value
        g_parts[pl.ds(i * each, each)] = split(value).reshape(each, bsize, 2 * LANES)
        return carry

    lax.fori_loop(0, chunks, begin, 0)
    x[at_sh : at_sh + shard, :] = w0_ref[rows(me_d * shard, shard), :]

    x[at_link:, :] = halves(dot(shared_cols[...], split(w0_ref[...])))

    for step in range(1, n_dom):
        dom_copy(SETUP, step, set_send.at[dom_peer(step)], set_recv.at[dom_source(step)]).wait_recv()
    for o in range(n_dom):
        for h in range(per_owner):
            at = o * per_owner + h
            table[at : at + 1, :] = set_recv[o, h : h + 1, :]
    table2_t[...] = table[...].T
    sums = [jnp.zeros((LANES, LANES), F32) for a in range(shard_chunks)]
    crowd = jnp.zeros((1, LANES), F32)
    for o in range(n_dom):
        crowd = jnp.maximum(crowd, set_recv[o, 4:5, :])
        for h in range(per_owner):
            i = o * per_owner + h
            held_row = set_recv[o, h : h + 1, :].astype(jnp.int32)
            held_col = table2_t[:, i : i + 1].astype(jnp.int32)
            for a in range(shard_chunks):
                here = (iota0 + LANES * a) == held_row
                sums[a] += jnp.where(here, set_recv[o, 2 + h : 3 + h, :], 0.0)
                own[LANES * a : LANES * (a + 1), LANES * i : LANES * (i + 1)] = ones_where(here)
                own_t[LANES * i : LANES * (i + 1), LANES * a : LANES * (a + 1)] = ones_where(
                    (iota1 + LANES * a) == held_col
                )
    for a in range(shard_chunks):
        total = column(COL_SHARED + 2 + a) + jnp.sum(sums[a], axis=1, keepdims=True)
        diag_sh[LANES * a : LANES * (a + 1), :] = jnp.broadcast_to(total, (LANES, LANES))
    flag_ref[0, 0] = jnp.max(crowd)

    def place_flows(vec):
        for t in range(nbuckets):
            at = slice(t * bucket_cap, (t + 1) * bucket_cap)
            flows = link_cond[at, :] * vec[at_link + at.start : at_link + at.stop, :]
            scatter_parts[t, :bucket_cap, :] = split(-flows)

    def apply_blocks(parts, out):
        def one(b, carry):
            other = block_link_ref[b]
            acc = dot(blocks[b, :, : 2 * bsize], jnp.concatenate([parts[b], parts[other]], axis=0))
            out[rows(b * bsize, bsize), :] = halves(acc[:bsize, :]) + acc[bsize:, :LANES]
            return carry

        lax.fori_loop(0, nblocks, one, 0, unroll=4)

    def apply(vec, parts, out, shifted=None):
        place_flows(vec)

        def one(b, carry):
            other = block_link_ref[b]
            at = rows(b * bsize, bsize)
            acc = dot(blocks[b], jnp.concatenate([parts[b], parts[other], scatter_parts[b // per_bucket]], axis=0))
            value = halves(acc[:bsize, :]) + acc[bsize:, :LANES]
            if shifted is not None:
                value = value - SHIFT * vec[at, :]
                shifted[b] = split(value)
            out[at, :] = value
            return carry

        lax.fori_loop(0, nblocks, one, 0, unroll=4)

    def gather_flow(parts):
        blocks_in = bucket_nodes // bsize
        for t in range(nbuckets):
            at = slice(t * bucket_cap, (t + 1) * bucket_cap)
            chunk = parts[t * blocks_in : (t + 1) * blocks_in].reshape(bucket_nodes, 2 * LANES)
            value = halves(dot(node_cols[at, :], chunk)) * link_cond[at, :]
            flow_parts[at, :] = split(value)

    def start_exchange(kind):
        for step in far_first:
            dom_copy(
                kind,
                step,
                stage.at[kind, dom_peer(step), pl.ds(0, cap)],
                recv.at[kind, me_d, pl.ds(0, cap)],
            ).start()
        recv[kind, me_d] = stage[kind, me_d]

    def wait_exchange(kind, receive):
        for step in range(1, n_dom):
            copy = dom_copy(
                kind,
                step,
                stage.at[kind, dom_peer(step), pl.ds(0, cap)],
                recv.at[kind, dom_source(step), pl.ds(0, cap)],
            )
            if receive:
                copy.wait_recv()
            else:
                copy.wait_send()

    def fill_stage(kind, matrix, value_parts):
        some = n_dom // 2

        def one(i, carry):
            got = halves(dot(matrix[rows(i * some * width, some * width), :], value_parts))
            stage[kind, pl.ds(i * some, some)] = got.reshape(some, width, LANES)
            return carry

        lax.fori_loop(0, 2, one, 0)
        start_exchange(kind)

    def send_flow(kind, parts):
        gather_flow(parts)
        fill_stage(kind, pack, flow_parts[...])

    def load_slots(kind):
        for o in range(n_dom):
            slot_parts[o * width : (o + 1) * width, :] = split(recv[kind, o])

    def collect_flow(kind):
        wait_exchange(kind, True)
        load_slots(kind)
        return halves(dot(own[...], slot_parts[...]))

    def send_back(kind, value):
        fill_stage(kind, own_t, split(value))

    def take_back(kind, out):
        wait_exchange(kind, True)
        load_slots(kind)
        out[at_link : at_link + links, :] = halves(dot(unpack[...], slot_parts[...]))

    def set_fixed(k):
        for i in range(chunks):
            at = slice(LANES * i, LANES * (i + 1))
            drive = amp_ref[at, :] * column(COL_SIN + chunks * k + i)
            fixed[at, :] = column(COL_MASS + i) * x[at, :] + drive
        for a in range(shard_chunks):
            at = slice(at_sh + LANES * a, at_sh + LANES * (a + 1))
            fixed[at, :] = column(COL_SHARED + a) * x[at, :]
        fixed[at_link:, :] = link_mass[...] * x[at_link:, :]

    def residual_nodes():
        def one(i, carry):
            at = rows(i * LANES, LANES)
            value = fixed[at, :] - jx[at, :] - nonlin_ref[...] * jnp.tanh(x[at, :])
            g[at, :] = value
            g_parts[pl.ds(i * each, each)] = split(value).reshape(each, bsize, 2 * LANES)
            return carry

        lax.fori_loop(0, chunks, one, 0)

    at = slice(at_sh, at_sh + shard)

    def residual_shared(where):
        g[where, :] = fixed[where, :] - jx[where, :]

    def shifted_shared():
        p[at, :] = (diag_sh[...] - SHIFT) * g[at, :] - collect_flow(FLOW_G)
        send_back(BACK_P, p[at, :])

    def start_shared():
        jx[at, :] = diag_sh[...] * x[at, :] - collect_flow(FLOW_P)
        send_back(BACK_Q, jx[at, :])
        residual_shared(at)
        shifted_shared()
        take_back(BACK_Q, jx)
        residual_shared(slice(at_link, at_link + links))
        for kind in (FLOW_P, BACK_Q):
            wait_exchange(kind, False)

    def newton(turn, carry):
        send_flow(FLOW_G, g_parts)
        pl.when(turn == 0)(start_shared)
        apply(g, g_parts, p, p_parts)
        send_flow(FLOW_P, p_parts)
        pl.when(turn > 0)(shifted_shared)

        def sum_over(i, sums, pairs):
            return tuple(
                s + jnp.sum((a * b).reshape(-1, 8, LANES), axis=0)
                for s, (a, b) in zip(sums, pairs)
            )

        def gram_early(i, sums):
            here = rows(i * LANES, LANES)
            vg, vp = g[here, :], p[here, :]
            return sum_over(i, sums, ((vg, vg), (vg, vp), (vp, vp)))

        size = 2 * LANES

        def gram_late(here, sums):
            vg, vp, vq = g[here, :], p[here, :], q[here, :]
            return sum_over(0, sums, ((vg, vq), (vp, vq), (vq, vq)))

        def place_and_gram(i, sums):
            here = rows(i * size, size)
            arriving = dot(node_rows[here, :], scatter_parts[i // (bucket_nodes // size)])
            q[here, :] = q[here, :] + halves(arriving)
            return gram_late(here, sums)

        zero = (jnp.zeros((8, LANES), F32),) * 3
        early = lax.fori_loop(0, chunks + shard_chunks, gram_early, zero)
        apply_blocks(p_parts, q)
        q[at, :] = diag_sh[...] * p[at, :] - collect_flow(FLOW_P)
        send_back(BACK_Q, q[at, :])
        late = gram_late(at, zero)
        take_back(BACK_P, p)
        place_flows(p)
        late = lax.fori_loop(0, nodes // size, place_and_gram, late)
        sums = early + late
        for i, s in enumerate(sums):
            gram_send[i : i + 1, :] = jnp.sum(s, axis=0, keepdims=True)
        gram_send[6:8, :] = jnp.zeros((2, LANES), F32)
        for step in far_first:
            dom_copy(GRAM, step, gram_send, gram_recv.at[me_d]).start()
        gram_recv[me_d] = gram_send[...]
        take_back(BACK_Q, q)
        for kind in (FLOW_G, FLOW_P, BACK_P, BACK_Q):
            wait_exchange(kind, False)
        for step in range(1, n_dom):
            copy = dom_copy(GRAM, step, gram_send, gram_recv.at[dom_source(step)])
            copy.wait_send()
            copy.wait_recv()
        total = gram_recv[0]
        for o in range(1, n_dom):
            total = total + gram_recv[o]
        gg, gp, pp, gq, pq, qq = [total[i : i + 1, :] for i in range(6)]
        norm2 = gg + 1e-30
        inv2 = 1.0 / norm2
        h00 = (gp + SHIFT * gg) * inv2
        turnover = h00 - SHIFT
        tail2 = pp - 2.0 * turnover * gp + turnover * turnover * gg
        inv_both = 1.0 / (jnp.sqrt(norm2) * jnp.sqrt(tail2))
        inv_tail2 = 1.0 / tail2
        push = turnover * SHIFT
        g_s = gq - turnover * gp - push * gg
        p_s = pq - turnover * pp - push * gp
        q_s = qq - turnover * pq - push * gq
        t_s = p_s - turnover * g_s
        s_s = q_s - turnover * p_s - push * g_s
        g_t = gp - turnover * gg
        h10 = tail2 * inv_both
        h01 = g_s * inv_both
        h11 = t_s * inv_tail2
        h21_2 = (
            s_s * inv_tail2
            - h01 * h01 * (2.0 - gg * inv2)
            - h11 * h11
            + 2.0 * h01 * h11 * g_t * inv_both
        )
        n11 = h00 * h00 + h10 * h10
        n12 = h00 * h01 + h10 * h11
        n22 = h01 * h01 + h11 * h11 + h21_2
        inv_det = 1.0 / (n11 * n22 - n12 * n12)
        c_p = norm2 * inv_both * (h01 * n11 - h00 * n12) * inv_det
        c_g = (h00 * n22 - h01 * n12) * inv_det - turnover * c_p

        def advance(here):
            vg, vp = g[here, :], p[here, :]
            x[here, :] = x[here, :] + c_g * vg + c_p * vp
            jx[here, :] = jx[here, :] + c_g * (vp + SHIFT * vg) + c_p * q[here, :]

        def one(i, carry):
            advance(rows(i * LANES, LANES))
            return carry

        lax.fori_loop(0, chunks + shard_chunks, one, 0)
        advance(slice(at_link, at_link + links))

        @pl.when(turn == NEWTON - 1)
        def _():
            set_fixed(1)

        @pl.when(turn < FINE * NEWTON - 1)
        def _():
            residual_nodes()
            residual_shared(slice(at_sh, at_link + links))

        return carry

    send_flow(FLOW_P, g_parts)
    apply(x, g_parts, jx)
    set_fixed(0)
    residual_nodes()
    lax.fori_loop(0, FINE * NEWTON, newton, 0)

    per_rows, per_shared = nodes // n_tm, shard // n_tm
    for a in range(shard_chunks):
        here = slice(at_sh + LANES * a, at_sh + LANES * (a + 1))
        start = w0_ref[rows(me_d * shard + LANES * a, LANES), :]
        jump = x[here, :] - column(COL_SHARED + 4 + a) * start
        pieces = LANES // per_shared
        for m in range(pieces):
            jump_sh_send[a * pieces + m] = jump[per_shared * m : per_shared * (m + 1), :]
    for step in range(1, n_tm):
        tm_copy(3, step, jump_sh_send.at[tm_peer(step)], jump_sh_recv.at[me_t]).start()
    jump_sh_recv[me_t] = jump_sh_send[me_t]
    for i in range(chunks):
        here = slice(LANES * i, LANES * (i + 1))
        jump_send[i] = x[here, :] - column(COL_GAIN + i) * x0_ref[here, :]
    pair_copy(1, jump_send.at[pl.ds(pairs * (1 - core), pairs)], pair_jump).start()
    pair_copy(0, gain_in_ref.at[pl.ds(pairs * (1 - core), pairs)], pair_gain).wait_recv()
    for step in range(1, n_tm):
        tm_copy(0, step, gain_send.at[tm_peer(step)], gain_recv.at[tm_source(step)]).wait_recv()
    for m in range(n_tm):
        table[m : m + 1, :] = gain_recv[m, 0:1, :]
        table[n_tm + m : n_tm + m + 1, :] = gain_recv[m, 1:2, :]
    first_core = core == 0
    own_gain, other_gain = gain_in_ref[pl.ds(pairs * core, pairs), :], pair_gain[...]
    table[2 * n_tm : 2 * n_tm + pairs, :] = jnp.where(first_core, own_gain, other_gain)
    table[3 * n_tm : 3 * n_tm + pairs, :] = jnp.where(first_core, other_gain, own_gain)
    table2_t[...] = table[...].T
    my_shared = rows(lax.rem(me_t, LANES // per_shared) * per_shared, per_shared)

    def map_copy(step, holder):
        return chip_copy(1, step, value_send.at[chip_peer(step)], jump_recv.at[holder])

    def value_copy(step, holder):
        return chip_copy(2, step, jump_recv.at[pairs + chip_peer(step)], value_recv.at[holder])

    def shared_copy(step, holder):
        return tm_copy(
            7, step, value_sh_send.at[tm_peer(step)], value_sh.at[rows(holder * per_shared, per_shared)]
        )

    def solve(gains, jumps, values):
        whole, total = gains[0], jumps[0]
        for m in range(1, len(gains)):
            whole = whole * gains[m]
            total = gains[m] * total + jumps[m]
        value = total / (1.0 - whole)
        for m in range(len(gains)):
            values[m] = value
            if m + 1 < len(gains):
                value = gains[m] * value + jumps[m]

    def pair_slices(i):
        mine, other = jump_send[pairs * core + i], pair_jump[i]
        return jnp.where(first_core, mine, other), jnp.where(first_core, other, mine)

    pair_copy(1, jump_send.at[pl.ds(pairs * (1 - core), pairs)], pair_jump).wait_recv()
    for i in range(pairs):
        first, second = pair_slices(i)
        value_send[i] = table2_t[:, 3 * n_tm + i : 3 * n_tm + i + 1] * first + second
    for step in far_chips:
        map_copy(step, chip).start()
    jump_recv[chip] = value_send[chip]
    for step in range(1, n_tm):
        tm_copy(3, step, jump_sh_send.at[tm_peer(step)], jump_sh_recv.at[tm_source(step)]).wait_recv()
    solve([table2_t[my_shared, n_tm + m : n_tm + m + 1] for m in range(n_tm)], jump_sh_recv, value_sh_send)
    for step in range(1, n_tm):
        shared_copy(step, me_t).start()
    value_sh[rows(me_t * per_shared, per_shared), :] = value_sh_send[me_t]
    for step in range(1, pairs):
        map_copy(step, chip_source(step)).wait_recv()
    pair_gains = [table2_t[:, 2 * k : 2 * k + 1] * table2_t[:, 2 * k + 1 : 2 * k + 2] for k in range(pairs)]
    solve(pair_gains, jump_recv, jump_recv.at[pl.ds(pairs, pairs)])
    for step in far_chips:
        value_copy(step, chip).start()
    value_recv[chip] = jump_recv[pairs + chip]
    for step in range(1, n_tm):
        shared_copy(step, tm_source(step)).wait_recv()
    for step in far_first:
        dom_copy(LAST, step, value_sh, out_sh_ref.at[rows(me_d * shard, shard)]).start()
    out_sh_ref[rows(me_d * shard, shard), :] = value_sh[...]
    for step in range(1, pairs):
        value_copy(step, chip_source(step)).wait_recv()
    half = nodes // 2
    for i in range(pairs):
        first, second = pair_slices(i)
        even = value_recv[i]
        odd = table2_t[:, 2 * n_tm + i : 2 * n_tm + i + 1] * even + first
        out_in_ref[rows(half * core + LANES * i, LANES), :] = jnp.where(first_core, even, odd)
        pair_value[LANES * i : LANES * (i + 1), :] = jnp.where(first_core, odd, even)
    pair_copy(2, pair_value, out_in_ref.at[rows(half * core, half)]).start()
    pair_copy(2, pair_value, out_in_ref.at[rows(half * (1 - core), half)]).wait_recv()
    for step in range(1, n_dom):
        copy = dom_copy(LAST, step, value_sh, out_sh_ref.at[rows(dom_source(step) * shard, shard)])
        copy.wait_recv()
        copy.wait_send()
        dom_copy(SETUP, step, set_send.at[dom_peer(step)], set_recv.at[me_d]).wait_send()
    for step in range(1, n_tm):
        tm_copy(0, step, gain_send.at[tm_peer(step)], gain_recv.at[me_t]).wait_send()
        tm_copy(3, step, jump_sh_send.at[tm_peer(step)], jump_sh_recv.at[me_t]).wait_send()
        shared_copy(step, me_t).wait_send()
    for step in range(1, pairs):
        map_copy(step, chip).wait_send()
        value_copy(step, chip).wait_send()
    pair_copy(0, gain_in_ref.at[pl.ds(pairs * (1 - core), pairs)], pair_gain).wait_send()
    pair_copy(1, jump_send.at[pl.ds(pairs * (1 - core), pairs)], pair_jump).wait_send()
    pair_copy(2, pair_value, out_in_ref.at[rows(half * core, half)]).wait_send()


def run(cap, width, bucket_nodes, bucket_cap, collective_id, n_tm, n_dom, operands):
    nodes, samples = operands[0].shape
    shared = operands[1].shape[0]
    shard = shared // n_dom
    nbuckets = nodes // bucket_nodes
    links = nbuckets * bucket_cap
    span = -(-bucket_cap // LANES) * LANES
    nblocks, bsize = operands[4].shape[0], operands[4].shape[1]
    total = nodes + shard + links
    slots = n_dom * width
    vmem = pl.BlockSpec(memory_space=pltpu.VMEM)
    smem = pl.BlockSpec(memory_space=pltpu.SMEM)
    specs = [vmem] * len(operands)
    specs[6] = smem
    for i in (0, 1, 4, 5, 13):
        specs[i] = pl.BlockSpec(memory_space=pl.ANY)
    state = pltpu.VMEM((total, samples), F32)
    tile = pltpu.VMEM((LANES, LANES), F32)
    return pl.pallas_call(
        functools.partial(kernel, cap, width, bucket_nodes, bucket_cap, n_tm, n_dom),
        out_shape=(
            jax.ShapeDtypeStruct((nodes, samples), F32),
            jax.ShapeDtypeStruct((shared, samples), F32),
            jax.ShapeDtypeStruct((1, 1), F32),
        ),
        in_specs=specs,
        out_specs=(vmem, vmem, smem),
        scratch_shapes=[
            pltpu.VMEM((nodes, samples), F32),
            pltpu.VMEM((shared, samples), F32),
            pltpu.VMEM((nblocks, bsize, bsize), F32),
            pltpu.VMEM((nblocks, bsize, bsize), F32),
            pltpu.VMEM((nodes, samples), F32),
            pltpu.SemaphoreType.DMA((5,)),
            state,
            state,
            state,
            state,
            state,
            state,
            pltpu.VMEM((nblocks, bsize, 2 * samples), BF16),
            pltpu.VMEM((nblocks, bsize, 2 * samples), BF16),
            pltpu.VMEM((links, 2 * samples), BF16),
            pltpu.VMEM((slots, 2 * samples), BF16),
            pltpu.VMEM((nblocks, 2 * bsize, 2 * bsize + span), BF16),
            pltpu.VMEM((links, bucket_nodes), BF16),
            pltpu.VMEM((nodes, span), BF16),
            pltpu.VMEM((nbuckets, 8, span), F32),
            pltpu.VMEM((nbuckets, span, 2 * samples), BF16),
            pltpu.VMEM((links, shared), BF16),
            pltpu.VMEM((slots, links), BF16),
            pltpu.VMEM((links, slots), BF16),
            pltpu.VMEM((shard, slots), BF16),
            pltpu.VMEM((slots, shard), BF16),
            tile,
            tile,
            tile,
            pltpu.VMEM((links, samples), F32),
            pltpu.VMEM((links, samples), F32),
            pltpu.VMEM((shard, samples), F32),
            pltpu.VMEM((4, n_dom, width, samples), F32),
            pltpu.VMEM((4, n_dom, width, samples), F32),
            pltpu.VMEM((n_dom, 8, LANES), F32),
            pltpu.VMEM((n_dom, 8, LANES), F32),
            pltpu.VMEM((n_tm, 8, LANES), F32),
            pltpu.VMEM((n_tm, 8, LANES), F32),
            pltpu.VMEM((8, LANES), F32),
            pltpu.VMEM((n_dom, 8, LANES), F32),
            pltpu.VMEM((n_tm, nodes // n_tm, samples), F32),
            pltpu.VMEM((n_tm, nodes // n_tm, samples), F32),
            pltpu.VMEM((n_tm, nodes // n_tm, samples), F32),
            pltpu.VMEM((n_tm, shard // n_tm, samples), F32),
            pltpu.VMEM((n_tm, shard // n_tm, samples), F32),
            pltpu.VMEM((n_tm, shard // n_tm, samples), F32),
            pltpu.VMEM((n_tm // 2, LANES), F32),
            pltpu.VMEM((n_tm // 2, LANES, samples), F32),
            pltpu.VMEM((nodes // 2, samples), F32),
            pltpu.VMEM((n_tm // 2, LANES, samples), F32),
            pltpu.VMEM((shard, samples), F32),
            pltpu.SemaphoreType.DMA((7, n_dom)),
            pltpu.SemaphoreType.DMA((7, n_dom)),
            pltpu.SemaphoreType.DMA((8, n_tm)),
            pltpu.SemaphoreType.DMA((8, n_tm)),
        ],
        compiler_params=pltpu.CompilerParams(
            collective_id=collective_id, has_side_effects=True, vmem_limit_bytes=62 * 1024 * 1024
        ),
        name="parareal",
    )(*operands)


def shards(
    state_interior,
    state_shared,
    gain_interior,
    gain_shared,
    jac_blocks,
    off_blocks,
    block_link,
    mass,
    shared_mass,
    shared_diag,
    link_node,
    link_shared,
    link_cond,
    source_amp,
    phase,
    nonlin,
):
    n_tm, n_dom = lax.axis_size("tm"), lax.axis_size("dom")

    def lanes(value):
        return value.reshape(-1, LANES)

    operands = (
        state_interior[0],
        state_shared[0],
        lanes(gain_interior),
        lanes(gain_shared),
        jac_blocks,
        off_blocks,
        block_link,
        lanes(mass),
        lanes(shared_mass),
        lanes(shared_diag),
        lanes(link_node),
        lanes(link_shared),
        lanes(link_cond),
        source_amp,
        lanes(phase),
        lanes(nonlin),
    )
    nodes, shard = state_interior.shape[1], state_shared.shape[1] // n_dom
    new_in, new_sh, crowd = run(SLOTS, LANES, 2 * LANES, SLOTS, 0, n_tm, n_dom, operands)
    new_in, new_sh = lax.cond(
        crowd[0, 0] < SLOTS,
        lambda: (new_in, new_sh),
        lambda: run(shard, shard, nodes, link_node.shape[0], 1, n_tm, n_dom, operands)[:2],
    )
    return (new_in[None], new_sh[None])


def solution(mesh):
    return jax.shard_map(
        shards,
        mesh=mesh,
        in_specs=(
            P("tm", "dom", None),
            P("tm", None, None),
            P("tm", "dom"),
            P("tm", None),
            P("dom", None, None),
            P("dom", None, None),
            P("dom"),
            P("dom"),
            P(),
            P(),
            P("dom"),
            P("dom"),
            P("dom"),
            P("dom", None),
            P("dom"),
            P(),
        ),
        out_specs=(P("tm", "dom", None), P("tm", None, None)),
        check_vma=False,
    )
```

```python
import functools
import math

import jax
import jax.numpy as jnp
from jax import lax
from jax.experimental import pallas as pl
from jax.experimental.pallas import tpu as pltpu
from jax.sharding import PartitionSpec as P

FINE = 2
NEWTON = 2
SHIFT = 8.0
SLOTS = 96
LANES = 128
MESH = pl.DeviceIdType.MESH
F32 = jnp.float32
BF16 = jnp.bfloat16

COL_MASS, COL_SIN, COL_GAIN, COL_SHARED, COL_NODE, COL_LINK, COL_COND = 0, 16, 48, 64, 72, 80, 88
ABSENT = 2.0**20
FLOW_G, FLOW_P, BACK_P, BACK_Q, SETUP, GRAM, LAST = range(7)


def halves(acc):
    return acc[:, :LANES] + acc[:, LANES:]


def split(value):
    high = value.astype(BF16)
    low = (value - high.astype(F32)).astype(BF16)
    return jnp.concatenate([high, low], axis=1)


def dot(a, b):
    return jnp.dot(a, b, preferred_element_type=F32)


def ones_where(mask):
    return jnp.where(mask, 1.0, 0.0).astype(BF16)


def kernel(
    cap,
    width,
    bucket_nodes,
    bucket_cap,
    n_tm,
    n_dom,
    x0_hbm,
    w0_hbm,
    gain_in_ref,
    gain_sh_ref,
    jac_hbm,
    off_hbm,
    block_link_ref,
    mass_ref,
    shared_mass_ref,
    shared_diag_ref,
    node_ref,
    link_ref,
    cond_ref,
    amp_hbm,
    phase_ref,
    nonlin_ref,
    out_in_ref,
    out_sh_ref,
    flag_ref,
    x0_ref,
    w0_ref,
    jac_ref,
    off_ref,
    amp_ref,
    load_sem,
    x,
    jx,
    g,
    p,
    q,
    fixed,
    g_parts,
    p_parts,
    flow_parts,
    slot_parts,
    blocks,
    node_cols,
    node_rows,
    bucket_rows,
    scatter_parts,
    shared_cols,
    pack,
    unpack,
    own,
    own_t,
    table,
    table_t,
    table2_t,
    link_mass,
    link_cond,
    diag_sh,
    stage,
    recv,
    set_send,
    set_recv,
    gain_send,
    gain_recv,
    gram_send,
    gram_recv,
    jump_send,
    jump_recv,
    value_send,
    jump_sh_send,
    jump_sh_recv,
    value_sh_send,
    pair_gain,
    pair_jump,
    pair_value,
    value_recv,
    value_sh,
    send_sem,
    recv_sem,
    tm_send,
    tm_recv,
):
    me_t, me_d = lax.axis_index("tm"), lax.axis_index("dom")
    nodes = x0_ref.shape[0]
    shard = w0_ref.shape[0] // n_dom
    links = flow_parts.shape[0]
    chunks, shard_chunks, link_chunks = nodes // LANES, shard // LANES, links // LANES
    at_sh, at_link = nodes, nodes + shard
    per_owner = width // LANES
    nblocks, bsize = jac_ref.shape[0], jac_ref.shape[1]
    iota0 = lax.broadcasted_iota(jnp.int32, (LANES, LANES), 0)
    iota1 = lax.broadcasted_iota(jnp.int32, (LANES, LANES), 1)

    def rows(start, size):
        return pl.ds(pl.multiple_of(start, size), size)

    def dom_peer(step):
        return lax.rem(me_d + step, n_dom)

    def dom_source(step):
        return lax.rem(me_d + n_dom - step, n_dom)

    def tm_peer(step):
        return lax.rem(me_t + step, n_tm)

    def tm_source(step):
        return lax.rem(me_t + n_tm - step, n_tm)

    def dom_copy(kind, step, source, target):
        return pltpu.make_async_remote_copy(
            src_ref=source,
            dst_ref=target,
            send_sem=send_sem.at[kind, step],
            recv_sem=recv_sem.at[kind, step],
            device_id={"dom": dom_peer(step)},
            device_id_type=MESH,
        )

    def tm_copy(kind, step, source, target):
        return pltpu.make_async_remote_copy(
            src_ref=source,
            dst_ref=target,
            send_sem=tm_send.at[kind, step],
            recv_sem=tm_recv.at[kind, step],
            device_id={"tm": tm_peer(step)},
            device_id_type=MESH,
        )

    pairs = n_tm // 2
    core, chip = lax.rem(me_t, 2), me_t // 2

    def pair_copy(kind, source, target):
        return pltpu.make_async_remote_copy(
            src_ref=source,
            dst_ref=target,
            send_sem=tm_send.at[4 + kind, 0],
            recv_sem=tm_recv.at[4 + kind, 0],
            device_id={"tm": me_t + 1 - 2 * core},
            device_id_type=MESH,
        )

    def chip_peer(step):
        return lax.rem(chip + step, pairs)

    def chip_source(step):
        return lax.rem(chip + pairs - step, pairs)

    def chip_copy(kind, step, source, target):
        return pltpu.make_async_remote_copy(
            src_ref=source,
            dst_ref=target,
            send_sem=tm_send.at[kind, step],
            recv_sem=tm_recv.at[kind, step],
            device_id={"tm": 2 * chip_peer(step) + core},
            device_id_type=MESH,
        )

    far_first = sorted(range(1, n_dom), key=lambda step: (step % 2 == 0, abs(2 * step - n_dom)))
    far_chips = sorted(range(1, pairs), key=lambda step: (step % 2 == 0, abs(2 * step - pairs)))

    loads = [
        pltpu.make_async_copy(source, target, load_sem.at[i])
        for i, (source, target) in enumerate(
            (
                (jac_hbm, jac_ref),
                (off_hbm, off_ref),
                (x0_hbm, x0_ref),
                (w0_hbm, w0_ref),
                (amp_hbm, amp_ref),
            )
        )
    ]
    for load in loads:
        load.start()

    if cap < width:
        for kind in range(4):
            for o in range(n_dom):
                recv[kind, o, cap:, :] = jnp.zeros((width - cap, LANES), F32)
    barrier = pltpu.get_barrier_semaphore()
    for step in range(1, n_dom):
        pl.semaphore_signal(barrier, inc=1, device_id={"dom": dom_peer(step)}, device_id_type=MESH)
    for step in range(1, n_tm):
        pl.semaphore_signal(barrier, inc=1, device_id={"tm": tm_peer(step)}, device_id_type=MESH)

    slice_f = me_t.astype(F32)
    table[...] = jnp.zeros((LANES, LANES), F32)
    table[COL_MASS : COL_MASS + chunks, :] = mass_ref[...]
    for k in range(FINE):
        angle = (slice_f * FINE + (k + 1.0)) * (2.0 * math.pi / (n_tm * FINE))
        at = COL_SIN + chunks * k
        table[at : at + chunks, :] = jnp.sin(angle + phase_ref[...])
    table[COL_GAIN : COL_GAIN + chunks, :] = gain_in_ref[...]
    for a in range(shard_chunks):
        row = shard_chunks * me_d + a
        table[COL_SHARED + a : COL_SHARED + a + 1, :] = shared_mass_ref[pl.ds(row, 1), :]
        table[COL_SHARED + 2 + a : COL_SHARED + 3 + a, :] = shared_diag_ref[pl.ds(row, 1), :]
        table[COL_SHARED + 4 + a : COL_SHARED + 5 + a, :] = gain_sh_ref[pl.ds(row, 1), :]
    given = node_ref.shape[0]
    table[COL_NODE : COL_NODE + given, :] = node_ref[...].astype(F32)
    table[COL_LINK : COL_LINK + given, :] = link_ref[...].astype(F32)
    table[COL_COND : COL_COND + given, :] = cond_ref[...]
    table_t[...] = table[...].T

    def column(at):
        return table_t[:, at : at + 1]

    nbuckets = nodes // bucket_nodes
    bucket_rows[...] = jnp.zeros(bucket_rows.shape, F32)
    crowd = jnp.zeros((1, 1), F32)
    if nbuckets == 1:
        for j in range(given):
            across = slice(LANES * j, LANES * (j + 1))
            bucket_rows[0, 0:1, across] = node_ref[j : j + 1, :].astype(F32)
            bucket_rows[0, 1:2, across] = cond_ref[j : j + 1, :]
        table[0:given, :] = node_ref[...].astype(F32)
        table[8 : 8 + given, :] = link_ref[...].astype(F32)
        table[16 : 16 + given, :] = cond_ref[...]
    else:
        given_node = [column(COL_NODE + j) for j in range(given)]
        given_link = [column(COL_LINK + j) for j in range(given)]
        given_cond = [column(COL_COND + j) for j in range(given)]
        bucket_col = [v.astype(jnp.int32) // bucket_nodes for v in given_node]
        bucket_row = [node_ref[j : j + 1, :] // bucket_nodes for j in range(given)]
        place = []
        for j in range(given):
            rank = jnp.zeros((LANES, 1), F32)
            for i in range(j + 1):
                same = bucket_col[j] == bucket_row[i]
                if i == j:
                    same = same & (iota1 < iota0)
                rank += jnp.sum(jnp.where(same, 1.0, 0.0), axis=1, keepdims=True)
            crowd = jnp.maximum(crowd, jnp.max(rank, axis=0, keepdims=True))
            place.append((bucket_col[j], rank.astype(jnp.int32)))

        def picked(masks, values, none):
            total = jnp.zeros((1, LANES), F32)
            for mask, value in zip(masks, values):
                total += jnp.sum(jnp.where(mask, value + none, 0.0), axis=0, keepdims=True)
            return total - none

        for i in range(nbuckets):
            masks = [(b == i) & (iota1 == r) for b, r in place]
            bucket_rows[i, 0:1, :] = picked(masks, given_node, ABSENT)
            bucket_rows[i, 1:2, :] = picked(masks, given_cond, 0.0)
        for i in range(link_chunks):
            masks = [(iota1 + LANES * i) == b * bucket_cap + r for b, r in place]
            table[i : i + 1, :] = picked(masks, given_node, ABSENT)
            table[8 + i : 9 + i, :] = picked(masks, given_link, ABSENT)
            table[16 + i : 17 + i, :] = picked(masks, given_cond, 0.0)
    table2_t[...] = table[...].T

    link_col = [table2_t[:, 8 + j : 9 + j].astype(jnp.int32) for j in range(link_chunks)]
    link_row = [table[8 + j : 9 + j, :].astype(jnp.int32) for j in range(link_chunks)]
    if cap == width:
        slot_col, slot_row = link_col, link_row
    else:
        owner_col = [v // shard for v in link_col]
        owner_row = [v // shard for v in link_row]
        slot_col, slot_row = [], []
        for j in range(link_chunks):
            rank_row = jnp.zeros((1, LANES), F32)
            rank_col = jnp.zeros((LANES, 1), F32)
            for i in range(j + 1):
                same_row = owner_col[i] == owner_row[j]
                same_col = owner_col[j] == owner_row[i]
                if i == j:
                    same_row = same_row & (iota0 < iota1)
                    same_col = same_col & (iota1 < iota0)
                rank_row += jnp.sum(jnp.where(same_row, 1.0, 0.0), axis=0, keepdims=True)
                rank_col += jnp.sum(jnp.where(same_col, 1.0, 0.0), axis=1, keepdims=True)
            real = jnp.where(owner_col[j] >= 0, rank_col, 0.0)
            crowd = jnp.maximum(crowd, jnp.max(real, axis=0, keepdims=True))
            slot_row.append(owner_row[j] * width + rank_row.astype(jnp.int32))
            slot_col.append(owner_col[j] * width + rank_col.astype(jnp.int32))
    link_cond_col = [table2_t[:, 16 + j : 17 + j] for j in range(link_chunks)]
    set_send[...] = jnp.zeros(set_send.shape, F32)
    for i in range(n_dom * per_owner):
        held = jnp.full((1, LANES), -1.0, F32)
        total = jnp.zeros((1, LANES), F32)
        for j in range(link_chunks):
            here = (iota1 + LANES * i) == slot_col[j]
            local = (link_col[j] % shard).astype(F32)
            held = jnp.maximum(held, jnp.max(jnp.where(here, local, -1.0), axis=0, keepdims=True))
            total += jnp.sum(jnp.where(here, link_cond_col[j], 0.0), axis=0, keepdims=True)
            unpack[LANES * j : LANES * (j + 1), LANES * i : LANES * (i + 1)] = ones_where(here)
            pack[LANES * i : LANES * (i + 1), LANES * j : LANES * (j + 1)] = ones_where(
                (iota0 + LANES * i) == slot_row[j]
            )
        o, h = i // per_owner, i % per_owner
        set_send[o, h : h + 1, :] = held
        set_send[o, 2 + h : 3 + h, :] = total
    for o in range(n_dom):
        set_send[o, 4:5, :] = jnp.broadcast_to(crowd, (1, LANES))
    gain_send[...] = jnp.zeros(gain_send.shape, F32)
    for m in range(n_tm):
        chunk = pairs * (m % 2) + m // 2
        gain_send[m, 0:1, :] = gain_in_ref[chunk : chunk + 1, :]
        row = shard_chunks * me_d + m * shard_chunks // n_tm
        gain_send[m, 1:2, :] = gain_sh_ref[pl.ds(row, 1), :]

    pl.semaphore_wait(barrier, n_dom - 1 + n_tm - 1)
    for step in range(1, n_dom):
        dom_copy(SETUP, step, set_send.at[dom_peer(step)], set_recv.at[me_d]).start()
    for step in range(1, n_tm):
        tm_copy(0, step, gain_send.at[tm_peer(step)], gain_recv.at[me_t]).start()
    pair_copy(0, gain_in_ref.at[pl.ds(pairs * (1 - core), pairs)], pair_gain).start()
    set_recv[me_d] = set_send[me_d]
    gain_recv[me_t] = gain_send[me_t]

    lanes_of = lax.broadcasted_iota(jnp.int32, (LANES, bucket_nodes), 1)
    for j in range(link_chunks):
        across = slice(LANES * j, LANES * (j + 1))
        node_col = table2_t[:, j : j + 1].astype(jnp.int32)
        local = jnp.where(node_col >= 0, node_col % bucket_nodes, -1)
        node_cols[across, :] = ones_where(lanes_of == local)
        link_cond[across, :] = jnp.broadcast_to(link_cond_col[j], (LANES, LANES))
        mass_sum = jnp.zeros((LANES, LANES), F32)
        for i in range(w0_ref.shape[0] // LANES):
            here = iota1 + LANES * i == link_col[j]
            mass_sum += jnp.where(here, shared_mass_ref[i : i + 1, :], 0.0)
            shared_cols[across, LANES * i : LANES * (i + 1)] = ones_where(here)
        link_mass[across, :] = jnp.broadcast_to(jnp.sum(mass_sum, axis=1, keepdims=True), (LANES, LANES))
    span = bucket_rows.shape[2]
    block_iota = lax.broadcasted_iota(jnp.int32, (bsize, span), 0).astype(F32)
    eye = lax.broadcasted_iota(jnp.int32, (bsize, bsize), 0) == lax.broadcasted_iota(jnp.int32, (bsize, bsize), 1)
    scatter_parts[...] = jnp.zeros(scatter_parts.shape, BF16)
    per_bucket = bucket_nodes // bsize

    for load in loads:
        load.wait()

    def cut(b, carry):
        held = bucket_rows[b // per_bucket]
        here = (block_iota + (b * bsize).astype(F32)) == held[0:1, :]
        own_cond = jnp.sum(jnp.where(here, held[1:2, :], 0.0), axis=1, keepdims=True)
        both = jnp.concatenate([jac_ref[b] + jnp.where(eye, own_cond, 0.0), off_ref[b]], axis=1)
        parts = split(both)
        blocks[b, :bsize, : 2 * bsize] = parts[:, :LANES]
        blocks[b, bsize:, : 2 * bsize] = parts[:, LANES:]
        places = ones_where(here)
        blocks[b, :bsize, 2 * bsize :] = places
        node_rows[rows(b * bsize, bsize), :] = places
        blocks[b, bsize:, 2 * bsize :] = jnp.zeros((bsize, span), BF16)
        return carry

    lax.fori_loop(0, nblocks, cut, 0, unroll=2)

    each = LANES // bsize

    def begin(i, carry):
        at = rows(i * LANES, LANES)
        value = x0_ref[at, :]
        x[at, :] = value
        g_parts[pl.ds(i * each, each)] = split(value).reshape(each, bsize, 2 * LANES)
        return carry

    lax.fori_loop(0, chunks, begin, 0)
    x[at_sh : at_sh + shard, :] = w0_ref[rows(me_d * shard, shard), :]

    x[at_link:, :] = halves(dot(shared_cols[...], split(w0_ref[...])))

    for step in range(1, n_dom):
        dom_copy(SETUP, step, set_send.at[dom_peer(step)], set_recv.at[dom_source(step)]).wait_recv()
    for o in range(n_dom):
        for h in range(per_owner):
            at = o * per_owner + h
            table[at : at + 1, :] = set_recv[o, h : h + 1, :]
    table2_t[...] = table[...].T
    sums = [jnp.zeros((LANES, LANES), F32) for a in range(shard_chunks)]
    crowd = jnp.zeros((1, LANES), F32)
    for o in range(n_dom):
        crowd = jnp.maximum(crowd, set_recv[o, 4:5, :])
        for h in range(per_owner):
            i = o * per_owner + h
            held_row = set_recv[o, h : h + 1, :].astype(jnp.int32)
            held_col = table2_t[:, i : i + 1].astype(jnp.int32)
            for a in range(shard_chunks):
                here = (iota0 + LANES * a) == held_row
                sums[a] += jnp.where(here, set_recv[o, 2 + h : 3 + h, :], 0.0)
                own[LANES * a : LANES * (a + 1), LANES * i : LANES * (i + 1)] = ones_where(here)
                own_t[LANES * i : LANES * (i + 1), LANES * a : LANES * (a + 1)] = ones_where(
                    (iota1 + LANES * a) == held_col
                )
    for a in range(shard_chunks):
        total = column(COL_SHARED + 2 + a) + jnp.sum(sums[a], axis=1, keepdims=True)
        diag_sh[LANES * a : LANES * (a + 1), :] = jnp.broadcast_to(total, (LANES, LANES))
    flag_ref[0, 0] = jnp.max(crowd)

    def place_flows(vec):
        for t in range(nbuckets):
            at = slice(t * bucket_cap, (t + 1) * bucket_cap)
            flows = link_cond[at, :] * vec[at_link + at.start : at_link + at.stop, :]
            scatter_parts[t, :bucket_cap, :] = split(-flows)

    def apply_blocks(parts, out):
        def one(b, carry):
            other = block_link_ref[b]
            acc = dot(blocks[b, :, : 2 * bsize], jnp.concatenate([parts[b], parts[other]], axis=0))
            out[rows(b * bsize, bsize), :] = halves(acc[:bsize, :]) + acc[bsize:, :LANES]
            return carry

        lax.fori_loop(0, nblocks, one, 0, unroll=4)

    def apply(vec, parts, out, shifted=None):
        place_flows(vec)

        def one(b, carry):
            other = block_link_ref[b]
            at = rows(b * bsize, bsize)
            acc = dot(blocks[b], jnp.concatenate([parts[b], parts[other], scatter_parts[b // per_bucket]], axis=0))
            value = halves(acc[:bsize, :]) + acc[bsize:, :LANES]
            if shifted is not None:
                value = value - SHIFT * vec[at, :]
                shifted[b] = split(value)
            out[at, :] = value
            return carry

        lax.fori_loop(0, nblocks, one, 0, unroll=4)

    def gather_flow(parts):
        blocks_in = bucket_nodes // bsize
        for t in range(nbuckets):
            at = slice(t * bucket_cap, (t + 1) * bucket_cap)
            chunk = parts[t * blocks_in : (t + 1) * blocks_in].reshape(bucket_nodes, 2 * LANES)
            value = halves(dot(node_cols[at, :], chunk)) * link_cond[at, :]
            flow_parts[at, :] = split(value)

    def start_exchange(kind):
        for step in far_first:
            dom_copy(
                kind,
                step,
                stage.at[kind, dom_peer(step), pl.ds(0, cap)],
                recv.at[kind, me_d, pl.ds(0, cap)],
            ).start()
        recv[kind, me_d] = stage[kind, me_d]

    def wait_exchange(kind, receive):
        for step in range(1, n_dom):
            copy = dom_copy(
                kind,
                step,
                stage.at[kind, dom_peer(step), pl.ds(0, cap)],
                recv.at[kind, dom_source(step), pl.ds(0, cap)],
            )
            if receive:
                copy.wait_recv()
            else:
                copy.wait_send()

    def fill_stage(kind, matrix, value_parts):
        some = n_dom // 2

        def one(i, carry):
            got = halves(dot(matrix[rows(i * some * width, some * width), :], value_parts))
            stage[kind, pl.ds(i * some, some)] = got.reshape(some, width, LANES)
            return carry

        lax.fori_loop(0, 2, one, 0)
        start_exchange(kind)

    def send_flow(kind, parts):
        gather_flow(parts)
        fill_stage(kind, pack, flow_parts[...])

    def load_slots(kind):
        for o in range(n_dom):
            slot_parts[o * width : (o + 1) * width, :] = split(recv[kind, o])

    def collect_flow(kind):
        wait_exchange(kind, True)
        load_slots(kind)
        return halves(dot(own[...], slot_parts[...]))

    def send_back(kind, value):
        fill_stage(kind, own_t, split(value))

    def take_back(kind, out):
        wait_exchange(kind, True)
        load_slots(kind)
        out[at_link : at_link + links, :] = halves(dot(unpack[...], slot_parts[...]))

    def set_fixed(k):
        for i in range(chunks):
            at = slice(LANES * i, LANES * (i + 1))
            drive = amp_ref[at, :] * column(COL_SIN + chunks * k + i)
            fixed[at, :] = column(COL_MASS + i) * x[at, :] + drive
        for a in range(shard_chunks):
            at = slice(at_sh + LANES * a, at_sh + LANES * (a + 1))
            fixed[at, :] = column(COL_SHARED + a) * x[at, :]
        fixed[at_link:, :] = link_mass[...] * x[at_link:, :]

    def residual_nodes():
        def one(i, carry):
            at = rows(i * LANES, LANES)
            value = fixed[at, :] - jx[at, :] - nonlin_ref[...] * jnp.tanh(x[at, :])
            g[at, :] = value
            g_parts[pl.ds(i * each, each)] = split(value).reshape(each, bsize, 2 * LANES)
            return carry

        lax.fori_loop(0, chunks, one, 0, unroll=4)

    at = slice(at_sh, at_sh + shard)

    def residual_shared(where):
        g[where, :] = fixed[where, :] - jx[where, :]

    def shifted_shared():
        p[at, :] = (diag_sh[...] - SHIFT) * g[at, :] - collect_flow(FLOW_G)
        send_back(BACK_P, p[at, :])

    def start_shared():
        jx[at, :] = diag_sh[...] * x[at, :] - collect_flow(FLOW_P)
        send_back(BACK_Q, jx[at, :])
        residual_shared(at)
        shifted_shared()
        take_back(BACK_Q, jx)
        residual_shared(slice(at_link, at_link + links))
        for kind in (FLOW_P, BACK_Q):
            wait_exchange(kind, False)

    def newton(turn, carry):
        send_flow(FLOW_G, g_parts)
        pl.when(turn == 0)(start_shared)
        apply(g, g_parts, p, p_parts)
        send_flow(FLOW_P, p_parts)
        pl.when(turn > 0)(shifted_shared)

        def sum_over(i, sums, pairs):
            return tuple(
                s + jnp.sum((a * b).reshape(-1, 8, LANES), axis=0)
                for s, (a, b) in zip(sums, pairs)
            )

        def gram_early(i, sums):
            here = rows(i * LANES, LANES)
            vg, vp = g[here, :], p[here, :]
            return sum_over(i, sums, ((vg, vg), (vg, vp), (vp, vp)))

        size = 2 * LANES

        def gram_late(here, sums):
            vg, vp, vq = g[here, :], p[here, :], q[here, :]
            return sum_over(0, sums, ((vg, vq), (vp, vq), (vq, vq)))

        def place_and_gram(i, sums):
            here = rows(i * size, size)
            arriving = dot(node_rows[here, :], scatter_parts[i // (bucket_nodes // size)])
            q[here, :] = q[here, :] + halves(arriving)
            return gram_late(here, sums)

        zero = (jnp.zeros((8, LANES), F32),) * 3
        early = lax.fori_loop(0, chunks + shard_chunks, gram_early, zero)
        apply_blocks(p_parts, q)
        q[at, :] = diag_sh[...] * p[at, :] - collect_flow(FLOW_P)
        send_back(BACK_Q, q[at, :])
        late = gram_late(at, zero)
        take_back(BACK_P, p)
        place_flows(p)
        late = lax.fori_loop(0, nodes // size, place_and_gram, late, unroll=2)
        sums = early + late
        for i, s in enumerate(sums):
            gram_send[i : i + 1, :] = jnp.sum(s, axis=0, keepdims=True)
        gram_send[6:8, :] = jnp.zeros((2, LANES), F32)
        for step in far_first:
            dom_copy(GRAM, step, gram_send, gram_recv.at[me_d]).start()
        gram_recv[me_d] = gram_send[...]
        take_back(BACK_Q, q)
        for kind in (FLOW_G, FLOW_P, BACK_P, BACK_Q):
            wait_exchange(kind, False)
        for step in range(1, n_dom):
            copy = dom_copy(GRAM, step, gram_send, gram_recv.at[dom_source(step)])
            copy.wait_send()
            copy.wait_recv()
        total = gram_recv[0]
        for o in range(1, n_dom):
            total = total + gram_recv[o]
        gg, gp, pp, gq, pq, qq = [total[i : i + 1, :] for i in range(6)]
        norm2 = gg + 1e-30
        inv2 = 1.0 / norm2
        h00 = (gp + SHIFT * gg) * inv2
        turnover = h00 - SHIFT
        tail2 = pp - 2.0 * turnover * gp + turnover * turnover * gg
        inv_both = 1.0 / (jnp.sqrt(norm2) * jnp.sqrt(tail2))
        inv_tail2 = 1.0 / tail2
        push = turnover * SHIFT
        g_s = gq - turnover * gp - push * gg
        p_s = pq - turnover * pp - push * gp
        q_s = qq - turnover * pq - push * gq
        t_s = p_s - turnover * g_s
        s_s = q_s - turnover * p_s - push * g_s
        g_t = gp - turnover * gg
        h10 = tail2 * inv_both
        h01 = g_s * inv_both
        h11 = t_s * inv_tail2
        h21_2 = (
            s_s * inv_tail2
            - h01 * h01 * (2.0 - gg * inv2)
            - h11 * h11
            + 2.0 * h01 * h11 * g_t * inv_both
        )
        n11 = h00 * h00 + h10 * h10
        n12 = h00 * h01 + h10 * h11
        n22 = h01 * h01 + h11 * h11 + h21_2
        inv_det = 1.0 / (n11 * n22 - n12 * n12)
        c_p = norm2 * inv_both * (h01 * n11 - h00 * n12) * inv_det
        c_g = (h00 * n22 - h01 * n12) * inv_det - turnover * c_p

        def advance(here):
            vg, vp = g[here, :], p[here, :]
            x[here, :] = x[here, :] + c_g * vg + c_p * vp
            jx[here, :] = jx[here, :] + c_g * (vp + SHIFT * vg) + c_p * q[here, :]

        def one(i, carry):
            advance(rows(i * LANES, LANES))
            return carry

        lax.fori_loop(0, chunks + shard_chunks, one, 0, unroll=3)
        advance(slice(at_link, at_link + links))

        @pl.when(turn == NEWTON - 1)
        def _():
            set_fixed(1)

        @pl.when(turn < FINE * NEWTON - 1)
        def _():
            residual_nodes()
            residual_shared(slice(at_sh, at_link + links))

        return carry

    send_flow(FLOW_P, g_parts)
    apply(x, g_parts, jx)
    set_fixed(0)
    residual_nodes()
    lax.fori_loop(0, FINE * NEWTON, newton, 0)

    per_rows, per_shared = nodes // n_tm, shard // n_tm
    for a in range(shard_chunks):
        here = slice(at_sh + LANES * a, at_sh + LANES * (a + 1))
        start = w0_ref[rows(me_d * shard + LANES * a, LANES), :]
        jump = x[here, :] - column(COL_SHARED + 4 + a) * start
        pieces = LANES // per_shared
        for m in range(pieces):
            jump_sh_send[a * pieces + m] = jump[per_shared * m : per_shared * (m + 1), :]
    for step in range(1, n_tm):
        tm_copy(3, step, jump_sh_send.at[tm_peer(step)], jump_sh_recv.at[me_t]).start()
    jump_sh_recv[me_t] = jump_sh_send[me_t]
    for i in range(chunks):
        here = slice(LANES * i, LANES * (i + 1))
        jump_send[i] = x[here, :] - column(COL_GAIN + i) * x0_ref[here, :]
    pair_copy(1, jump_send.at[pl.ds(pairs * (1 - core), pairs)], pair_jump).start()
    pair_copy(0, gain_in_ref.at[pl.ds(pairs * (1 - core), pairs)], pair_gain).wait_recv()
    for step in range(1, n_tm):
        tm_copy(0, step, gain_send.at[tm_peer(step)], gain_recv.at[tm_source(step)]).wait_recv()
    for m in range(n_tm):
        table[m : m + 1, :] = gain_recv[m, 0:1, :]
        table[n_tm + m : n_tm + m + 1, :] = gain_recv[m, 1:2, :]
    first_core = core == 0
    own_gain, other_gain = gain_in_ref[pl.ds(pairs * core, pairs), :], pair_gain[...]
    table[2 * n_tm : 2 * n_tm + pairs, :] = jnp.where(first_core, own_gain, other_gain)
    table[3 * n_tm : 3 * n_tm + pairs, :] = jnp.where(first_core, other_gain, own_gain)
    table2_t[...] = table[...].T
    my_shared = rows(lax.rem(me_t, LANES // per_shared) * per_shared, per_shared)

    def map_copy(step, holder):
        return chip_copy(1, step, value_send.at[chip_peer(step)], jump_recv.at[holder])

    def value_copy(step, holder):
        return chip_copy(2, step, jump_recv.at[pairs + chip_peer(step)], value_recv.at[holder])

    def shared_copy(step, holder):
        return tm_copy(
            7, step, value_sh_send.at[tm_peer(step)], value_sh.at[rows(holder * per_shared, per_shared)]
        )

    def solve(gains, jumps, values):
        whole, total = gains[0], jumps[0]
        for m in range(1, len(gains)):
            whole = whole * gains[m]
            total = gains[m] * total + jumps[m]
        value = total / (1.0 - whole)
        for m in range(len(gains)):
            values[m] = value
            if m + 1 < len(gains):
                value = gains[m] * value + jumps[m]

    def pair_slices(i):
        mine, other = jump_send[pairs * core + i], pair_jump[i]
        return jnp.where(first_core, mine, other), jnp.where(first_core, other, mine)

    pair_copy(1, jump_send.at[pl.ds(pairs * (1 - core), pairs)], pair_jump).wait_recv()
    for i in range(pairs):
        first, second = pair_slices(i)
        value_send[i] = table2_t[:, 3 * n_tm + i : 3 * n_tm + i + 1] * first + second
    for step in far_chips:
        map_copy(step, chip).start()
    jump_recv[chip] = value_send[chip]
    for step in range(1, n_tm):
        tm_copy(3, step, jump_sh_send.at[tm_peer(step)], jump_sh_recv.at[tm_source(step)]).wait_recv()
    solve([table2_t[my_shared, n_tm + m : n_tm + m + 1] for m in range(n_tm)], jump_sh_recv, value_sh_send)
    for step in range(1, n_tm):
        shared_copy(step, me_t).start()
    value_sh[rows(me_t * per_shared, per_shared), :] = value_sh_send[me_t]
    for step in range(1, pairs):
        map_copy(step, chip_source(step)).wait_recv()
    pair_gains = [table2_t[:, 2 * k : 2 * k + 1] * table2_t[:, 2 * k + 1 : 2 * k + 2] for k in range(pairs)]
    solve(pair_gains, jump_recv, jump_recv.at[pl.ds(pairs, pairs)])
    for step in far_chips:
        value_copy(step, chip).start()
    value_recv[chip] = jump_recv[pairs + chip]
    for step in range(1, n_tm):
        shared_copy(step, tm_source(step)).wait_recv()
    for step in far_first:
        dom_copy(LAST, step, value_sh, out_sh_ref.at[rows(me_d * shard, shard)]).start()
    out_sh_ref[rows(me_d * shard, shard), :] = value_sh[...]
    for step in range(1, pairs):
        value_copy(step, chip_source(step)).wait_recv()
    half = nodes // 2
    for i in range(pairs):
        first, second = pair_slices(i)
        even = value_recv[i]
        odd = table2_t[:, 2 * n_tm + i : 2 * n_tm + i + 1] * even + first
        out_in_ref[rows(half * core + LANES * i, LANES), :] = jnp.where(first_core, even, odd)
        pair_value[LANES * i : LANES * (i + 1), :] = jnp.where(first_core, odd, even)
    pair_copy(2, pair_value, out_in_ref.at[rows(half * core, half)]).start()
    pair_copy(2, pair_value, out_in_ref.at[rows(half * (1 - core), half)]).wait_recv()
    for step in range(1, n_dom):
        copy = dom_copy(LAST, step, value_sh, out_sh_ref.at[rows(dom_source(step) * shard, shard)])
        copy.wait_recv()
        copy.wait_send()
        dom_copy(SETUP, step, set_send.at[dom_peer(step)], set_recv.at[me_d]).wait_send()
    for step in range(1, n_tm):
        tm_copy(0, step, gain_send.at[tm_peer(step)], gain_recv.at[me_t]).wait_send()
        tm_copy(3, step, jump_sh_send.at[tm_peer(step)], jump_sh_recv.at[me_t]).wait_send()
        shared_copy(step, me_t).wait_send()
    for step in range(1, pairs):
        map_copy(step, chip).wait_send()
        value_copy(step, chip).wait_send()
    pair_copy(0, gain_in_ref.at[pl.ds(pairs * (1 - core), pairs)], pair_gain).wait_send()
    pair_copy(1, jump_send.at[pl.ds(pairs * (1 - core), pairs)], pair_jump).wait_send()
    pair_copy(2, pair_value, out_in_ref.at[rows(half * core, half)]).wait_send()


def run(cap, width, bucket_nodes, bucket_cap, collective_id, n_tm, n_dom, operands):
    nodes, samples = operands[0].shape
    shared = operands[1].shape[0]
    shard = shared // n_dom
    nbuckets = nodes // bucket_nodes
    links = nbuckets * bucket_cap
    span = -(-bucket_cap // LANES) * LANES
    nblocks, bsize = operands[4].shape[0], operands[4].shape[1]
    total = nodes + shard + links
    slots = n_dom * width
    vmem = pl.BlockSpec(memory_space=pltpu.VMEM)
    smem = pl.BlockSpec(memory_space=pltpu.SMEM)
    specs = [vmem] * len(operands)
    specs[6] = smem
    for i in (0, 1, 4, 5, 13):
        specs[i] = pl.BlockSpec(memory_space=pl.ANY)
    state = pltpu.VMEM((total, samples), F32)
    tile = pltpu.VMEM((LANES, LANES), F32)
    return pl.pallas_call(
        functools.partial(kernel, cap, width, bucket_nodes, bucket_cap, n_tm, n_dom),
        out_shape=(
            jax.ShapeDtypeStruct((nodes, samples), F32),
            jax.ShapeDtypeStruct((shared, samples), F32),
            jax.ShapeDtypeStruct((1, 1), F32),
        ),
        in_specs=specs,
        out_specs=(vmem, vmem, smem),
        scratch_shapes=[
            pltpu.VMEM((nodes, samples), F32),
            pltpu.VMEM((shared, samples), F32),
            pltpu.VMEM((nblocks, bsize, bsize), F32),
            pltpu.VMEM((nblocks, bsize, bsize), F32),
            pltpu.VMEM((nodes, samples), F32),
            pltpu.SemaphoreType.DMA((5,)),
            state,
            state,
            state,
            state,
            state,
            state,
            pltpu.VMEM((nblocks, bsize, 2 * samples), BF16),
            pltpu.VMEM((nblocks, bsize, 2 * samples), BF16),
            pltpu.VMEM((links, 2 * samples), BF16),
            pltpu.VMEM((slots, 2 * samples), BF16),
            pltpu.VMEM((nblocks, 2 * bsize, 2 * bsize + span), BF16),
            pltpu.VMEM((links, bucket_nodes), BF16),
            pltpu.VMEM((nodes, span), BF16),
            pltpu.VMEM((nbuckets, 8, span), F32),
            pltpu.VMEM((nbuckets, span, 2 * samples), BF16),
            pltpu.VMEM((links, shared), BF16),
            pltpu.VMEM((slots, links), BF16),
            pltpu.VMEM((links, slots), BF16),
            pltpu.VMEM((shard, slots), BF16),
            pltpu.VMEM((slots, shard), BF16),
            tile,
            tile,
            tile,
            pltpu.VMEM((links, samples), F32),
            pltpu.VMEM((links, samples), F32),
            pltpu.VMEM((shard, samples), F32),
            pltpu.VMEM((4, n_dom, width, samples), F32),
            pltpu.VMEM((4, n_dom, width, samples), F32),
            pltpu.VMEM((n_dom, 8, LANES), F32),
            pltpu.VMEM((n_dom, 8, LANES), F32),
            pltpu.VMEM((n_tm, 8, LANES), F32),
            pltpu.VMEM((n_tm, 8, LANES), F32),
            pltpu.VMEM((8, LANES), F32),
            pltpu.VMEM((n_dom, 8, LANES), F32),
            pltpu.VMEM((n_tm, nodes // n_tm, samples), F32),
            pltpu.VMEM((n_tm, nodes // n_tm, samples), F32),
            pltpu.VMEM((n_tm, nodes // n_tm, samples), F32),
            pltpu.VMEM((n_tm, shard // n_tm, samples), F32),
            pltpu.VMEM((n_tm, shard // n_tm, samples), F32),
            pltpu.VMEM((n_tm, shard // n_tm, samples), F32),
            pltpu.VMEM((n_tm // 2, LANES), F32),
            pltpu.VMEM((n_tm // 2, LANES, samples), F32),
            pltpu.VMEM((nodes // 2, samples), F32),
            pltpu.VMEM((n_tm // 2, LANES, samples), F32),
            pltpu.VMEM((shard, samples), F32),
            pltpu.SemaphoreType.DMA((7, n_dom)),
            pltpu.SemaphoreType.DMA((7, n_dom)),
            pltpu.SemaphoreType.DMA((8, n_tm)),
            pltpu.SemaphoreType.DMA((8, n_tm)),
        ],
        compiler_params=pltpu.CompilerParams(
            collective_id=collective_id, has_side_effects=True, vmem_limit_bytes=62 * 1024 * 1024
        ),
        name="parareal",
    )(*operands)


def shards(
    state_interior,
    state_shared,
    gain_interior,
    gain_shared,
    jac_blocks,
    off_blocks,
    block_link,
    mass,
    shared_mass,
    shared_diag,
    link_node,
    link_shared,
    link_cond,
    source_amp,
    phase,
    nonlin,
):
    n_tm, n_dom = lax.axis_size("tm"), lax.axis_size("dom")

    def lanes(value):
        return value.reshape(-1, LANES)

    operands = (
        state_interior[0],
        state_shared[0],
        lanes(gain_interior),
        lanes(gain_shared),
        jac_blocks,
        off_blocks,
        block_link,
        lanes(mass),
        lanes(shared_mass),
        lanes(shared_diag),
        lanes(link_node),
        lanes(link_shared),
        lanes(link_cond),
        source_amp,
        lanes(phase),
        lanes(nonlin),
    )
    nodes, shard = state_interior.shape[1], state_shared.shape[1] // n_dom
    new_in, new_sh, crowd = run(SLOTS, LANES, 2 * LANES, SLOTS, 0, n_tm, n_dom, operands)
    new_in, new_sh = lax.cond(
        crowd[0, 0] < SLOTS,
        lambda: (new_in, new_sh),
        lambda: run(shard, shard, nodes, link_node.shape[0], 1, n_tm, n_dom, operands)[:2],
    )
    return (new_in[None], new_sh[None])


def solution(mesh):
    return jax.shard_map(
        shards,
        mesh=mesh,
        in_specs=(
            P("tm", "dom", None),
            P("tm", None, None),
            P("tm", "dom"),
            P("tm", None),
            P("dom", None, None),
            P("dom", None, None),
            P("dom"),
            P("dom"),
            P(),
            P(),
            P("dom"),
            P("dom"),
            P("dom"),
            P("dom", None),
            P("dom"),
            P(),
        ),
        out_specs=(P("tm", "dom", None), P("tm", None, None)),
        check_vma=False,
    )
```
